32 devices in a mesh: lat: 8 (over z, y), lev: 4 (over x, core).
Axes of the slice: x: 2, y: 2, z: 4, core: 2. Of those that a mesh axis runs over, the one named last changes fastest.
Arguments:
- tracer: float32 [2, 4, 384, 1152], P(None, 'lev', 'lat'), may hold values from 0.1 to 2
- east_courant: float32 [4, 384, 1152], P('lev', 'lat'), may hold values from -0.8 to 0.8
- north_courant: float32 [4, 384, 1152], P('lev', 'lat'), may hold values from -0.8 to 0.8
- fall_speed: float32 [2, 4, 384, 1152], P(None, 'lev', 'lat'), may hold values from 0.05 to 0.6
Outputs:
- tracer_out: float32 [2, 4, 384, 1152], P(None, 'lev', 'lat')
- deposit: float32 [2, 384, 1152], P(None, 'lat', 'lev')
The draws below stay inside these ranges and needn't reach their ends.
All inputs are finite; a program needn't handle non-finite values.
Results may differ from the reference program's by a relative error of at most 0.0003.
Values sent between devices are 32-bit elements; how exact they have to be, the bound alone decides.
No kernel may reach another device: no remote copies, remote signals or barrier semaphores. Data moves between devices by JAX's collectives and lax.ppermute only.
A program may use at most 64 MiB of HBM per device.

```python
import math
import jax
import jax.numpy as jnp
from jax import lax

BINS = 2
NLON = 1152
HSUB = 4
SETTLE_SUBSTEPS = 6
LEV = 4
NLAT = 384


def levels(rng, extent, pieces, smallest, largest):
    loudness, own = 1.0, jax.random.fold_in(rng, 6)
    for position, blocks in pieces:
        heights = jnp.exp(jax.random.uniform(jax.random.fold_in(own, position), (blocks,), jnp.float32, smallest / len(pieces), largest / len(pieces)))
        loudness = loudness * jnp.repeat(heights, extent[position] // blocks).reshape([-1 if axis == position else 1 for axis in range(len(extent))])
    return loudness


def setup_inputs(seed: int = 0) -> dict:
    key_of = jax.random.split(jax.random.key(seed), 5)
    return {
        "tracer": jnp.clip(0.1 + 1.9 * jax.random.uniform(key_of[0], (BINS, LEV, NLAT, NLON), jnp.float32) ** levels(key_of[0], (BINS, LEV, NLAT, NLON), ((1, 4), (2, 8)), -0.2, 0.2), 0.1, 2.0),
        "east_courant": jnp.clip(jax.random.uniform(key_of[1], (LEV, NLAT, NLON), jnp.float32, -0.8, 0.8) * levels(key_of[1], (LEV, NLAT, NLON), ((0, 4), (1, 8)), -0.4, 0.0), -0.8, 0.8),
        "north_courant": jnp.clip(jax.random.uniform(key_of[2], (LEV, NLAT, NLON), jnp.float32, -0.8, 0.8) * levels(key_of[2], (LEV, NLAT, NLON), ((0, 4), (1, 8)), -0.4, 0.0), -0.8, 0.8),
        "fall_speed": jnp.clip(jnp.exp(math.log(0.6) - 2.4849067 * jax.random.uniform(key_of[3], (BINS, LEV, NLAT, NLON), jnp.float32) ** levels(key_of[3], (BINS, LEV, NLAT, NLON), ((1, 4), (2, 8)), -0.2, 0.2)), 0.05, 0.6),
    }


def limiter_face_value(outer_west, inner_west, inner_east, outer_east):
    interp = (7.0 / 12.0) * (inner_west + inner_east) - (1.0 / 12.0) * (outer_west + outer_east)
    return jnp.clip(interp, jnp.minimum(inner_west, inner_east), jnp.maximum(inner_west, inner_east))


def window_for_cell(source, start, length, axis_dim):
    return lax.slice_in_dim(source, start, start + length, axis=axis_dim)


def sweep(halo_padded_field, courant, axis_dim):
    cells = halo_padded_field.shape[axis_dim] - 6
    faces = limiter_face_value(window_for_cell(halo_padded_field, 0, cells + 3, axis_dim), window_for_cell(halo_padded_field, 1, cells + 3, axis_dim),
                         window_for_cell(halo_padded_field, 2, cells + 3, axis_dim), window_for_cell(halo_padded_field, 3, cells + 3, axis_dim))
    middle = window_for_cell(halo_padded_field, 2, cells + 2, axis_dim)
    west_face = window_for_cell(faces, 0, cells + 2, axis_dim)
    east_face = window_for_cell(faces, 1, cells + 2, axis_dim)
    spread = east_face - west_face
    curvature = 6.0 * middle - 3.0 * (west_face + east_face)
    courant_abs = jnp.abs(courant)
    shape_term = 1.0 - (2.0 / 3.0) * courant_abs
    from_west = window_for_cell(east_face, 0, cells + 1, axis_dim) - 0.5 * courant_abs * (
        window_for_cell(spread, 0, cells + 1, axis_dim) - shape_term * window_for_cell(curvature, 0, cells + 1, axis_dim))
    from_east = window_for_cell(west_face, 1, cells + 1, axis_dim) + 0.5 * courant_abs * (
        window_for_cell(spread, 1, cells + 1, axis_dim) + shape_term * window_for_cell(curvature, 1, cells + 1, axis_dim))
    face_flux_values = courant * jnp.where(courant >= 0, from_west, from_east)
    return window_for_cell(halo_padded_field, 3, cells, axis_dim) - (window_for_cell(face_flux_values, 1, cells, axis_dim) - window_for_cell(face_flux_values, 0, cells, axis_dim))


def zonal(field, east_courant):
    last_dim = field.ndim - 1
    width = field.shape[last_dim]
    halo_padded_field = jnp.concatenate([window_for_cell(field, width - 3, 3, last_dim), field, window_for_cell(field, 0, 3, last_dim)], last_dim)
    cour_dim = east_courant.ndim - 1
    courant = jnp.concatenate([window_for_cell(east_courant, width - 1, 1, cour_dim), east_courant], cour_dim)
    return sweep(halo_padded_field, courant, last_dim)


def horizontal(field, east_courant, face_cour):
    field = zonal(field, east_courant)
    halo_padded_field = jnp.pad(field, ((0, 0), (3, 3), (0, 0)))
    return sweep(halo_padded_field, face_cour, 1)


def settle(column_mass, fall_speed):
    deposit = jnp.zeros_like(column_mass[:, 0])
    for settle_substep in range(SETTLE_SUBSTEPS):
        speeds = fall_speed * (1.0 + 0.5 * jnp.tanh(column_mass))
        face_flux_values = speeds * column_mass
        inflow = jnp.concatenate([jnp.zeros_like(face_flux_values[:, :1]), face_flux_values[:, :-1]], 1)
        column_mass = (column_mass + inflow) - face_flux_values
        deposit = deposit + face_flux_values[:, -1]
    return column_mass, deposit


def reference(tracer, east_courant, north_courant, fall_speed):
    row_ids = jnp.arange(NLAT, dtype=jnp.int32)
    north_faces = jnp.where((row_ids == NLAT - 1)[None, :, None], jnp.zeros_like(north_courant), north_courant)
    face_cour = jnp.concatenate([jnp.zeros_like(north_faces[:, :1]), north_faces], 1)

    def advect_many(inputs):
        field, east_level, face_level = inputs
        for settle_substep in range(HSUB):
            field = horizontal(field, east_level, face_level)
        return field

    def advect_once(inputs):
        field, east_level, face_level = inputs
        return horizontal(field, east_level, face_level)

    by_level = lax.map(advect_many, (jnp.moveaxis(tracer, 1, 0), east_courant, face_cour))
    settled, deposit = settle(jnp.moveaxis(by_level, 0, 1), fall_speed)
    closing = lax.map(advect_once, (jnp.moveaxis(settled, 1, 0), east_courant, face_cour))
    return jnp.moveaxis(closing, 0, 1), deposit
```

```python
import functools
import jax
import jax.numpy as jnp
from jax import lax
from jax.experimental import pallas as pl
from jax.experimental.pallas import tpu as pltpu
from jax.sharding import PartitionSpec as P

HSUB = 4
SETTLE_SUBSTEPS = 6
SUB = 8
LANE = 128
F32 = jnp.float32


def loop(count, body, unroll=1):
    def step(i, carry):
        body(i)
        return carry

    lax.fori_loop(0, count, step, 0, unroll=unroll)


def group(i):
    if isinstance(i, int):
        return pl.ds(SUB * i, SUB)
    return pl.ds(pl.multiple_of(SUB * i, SUB), SUB)


def roll(x, shift, axis):
    shift %= x.shape[axis]
    return pltpu.roll(x, shift, axis) if shift else x


def sublanes(width):
    return lax.broadcasted_iota(jnp.int32, (SUB, width), 0)


def lanes():
    return lax.broadcasted_iota(jnp.int32, (SUB, LANE), 1)


def coefficients(k):
    s = jnp.abs(k)
    r = 1.0 - s
    ks = k * s
    return k * (r * r), -(ks * r), ks * (3.0 - 2.0 * s)


def face(a, b, c, d):
    interp = (7.0 / 12.0) * (b + c) - (1.0 / 12.0) * (a + d)
    return jnp.minimum(jnp.maximum(interp, jnp.minimum(b, c)), jnp.maximum(b, c))


def swept(q, below2, below, above, co, axis):
    al, be, ga = co
    f = face(below2, below, q, above)
    up = al >= 0
    other = jnp.where(up, roll(f, 1, axis), roll(f, -1, axis))
    w = al * f + be * other + ga * jnp.where(up, below, q)
    return q - (roll(w, -1, axis) - w)


def zonal(q, co):
    return swept(q, roll(q, 2, 1), roll(q, 1, 1), roll(q, -1, 1), co, 1)


class Plan:
    def __init__(self, bins, rows, lons, count):
        self.bins, self.rows, self.lons, self.count = bins, rows, lons, count
        self.groups = rows // SUB
        self.width = lons // count
        self.full, self.rem = divmod(self.width, LANE)
        self.per = LANE // self.rem if self.rem else 1
        cores = bins * self.groups
        rems = (lambda n: -(-n // self.per)) if self.rem else (lambda n: 0)
        self.core_rem = cores * self.full
        self.core = self.core_rem + rems(cores)
        self.halo_rem = self.core + bins * self.full
        self.field = self.halo_rem + rems(bins)
        self.shared = bool(self.rem) and 2 * bins <= self.per
        self.speed_rem = self.field + bins * self.full
        self.total = self.speed_rem + (0 if self.shared else rems(bins))
        self.tiles = lons // LANE
        self.halo_groups = 2 * bins + 3 + (bins + 1) // 2


def window(tiles, start, width, at, cache):
    tile, off = divmod(start, LANE)

    def turned(i):
        key = (i, (at - off) % LANE)
        if key not in cache:
            cache[key] = roll(tiles[i], at - off, 1)
        return cache[key]

    if off + width <= LANE:
        return turned(tile)
    return jnp.where(lanes() < at + LANE - off, turned(tile), turned(tile + 1))


def pack(plan, rows_of, out, tile_at, first_rem):
    held = [None] * plan.count
    for i, tiles in enumerate(rows_of):
        slot = i % plan.per
        cache = {}
        for j in range(plan.count):
            base = j * plan.width
            for t in range(plan.full):
                v = window(tiles, base + LANE * t, LANE, 0, cache)
                out[j, group(tile_at(i) + t), :] = v
            if plan.rem:
                at = plan.rem * slot
                v = window(tiles, base + LANE * plan.full, plan.rem, at, cache)
                held[j] = v if slot == 0 else jnp.where(lanes() < at, held[j], v)
                if slot == plan.per - 1 or i == len(rows_of) - 1:
                    out[j, group(first_rem + i // plan.per), :] = held[j]


def unpack(plan, parts, index, rem_vector, slot):
    tiles = [None] * plan.tiles

    def put(v, start, width, at):
        tile, off = divmod(start, LANE)
        v = roll(v, off - at, 1)
        for t, low, high in ((tile, off, off + width), (tile + 1, 0, off + width - LANE)):
            if high > low:
                tiles[t] = v if low == 0 else jnp.where(lanes() < low, tiles[t], v)

    for j in range(plan.count):
        base = j * plan.width
        for t in range(plan.full):
            put(parts[j, group(index + t), :], base + LANE * t, LANE, 0)
        if plan.rem:
            put(parts[j, group(rem_vector), :], base + LANE * plan.full, plan.rem, plan.rem * slot)
    return tiles


def split(x):
    return [x[:, LANE * t : LANE * (t + 1)] for t in range(x.shape[1] // LANE)]


def start_kernel(plan, tracer, east, north, speed, q1, up, down):
    top, bins = plan.groups - 1, plan.bins
    sub = sublanes(plan.lons)

    def body(g):
        co = coefficients(roll(east[group(g), :], 1, 1))
        for b in range(bins):
            q1[b, group(g), :] = zonal(tracer[b, group(g), :], co)

    loop(plan.groups, body)
    for b in range(bins):
        for half in range(2):
            v = q1[b, group(top - 1 + half), :]
            if b == 0 and half == 0:
                v = jnp.where(sub == 0, roll(north[group(top - 1), :], -3, 0), v)
            up[group(2 * b + half), :] = v
            down[group(2 * b + half), :] = q1[b, group(half), :]
    base = 2 * bins
    up[group(base), :] = east[group(top), :]
    up[group(base + 1), :] = north[group(top), :]
    up[group(base + 2), :] = jnp.where(
        sub < 4, roll(east[group(top - 1), :], 4, 0), north[group(top - 1), :]
    )
    down[group(base), :] = east[group(0), :]
    down[group(base + 1), :] = north[group(0), :]
    down[group(base + 2), :] = jnp.where(sub < 4, east[group(1), :], roll(north[group(1), :], 4, 0))
    for p in range((bins + 1) // 2):
        other = min(2 * p + 1, bins - 1)
        up[group(base + 3 + p), :] = jnp.where(
            sub < 4, roll(speed[other, group(top), :], 4, 0), speed[2 * p, group(top), :]
        )
        down[group(base + 3 + p), :] = jnp.where(
            sub < 4, speed[2 * p, group(0), :], roll(speed[other, group(0), :], 4, 0)
        )


def speed_kernel(plan, speed, *refs):
    outs, chunks = refs[:-1], refs[-1]
    me = lax.axis_index("lev")
    rows_of = [
        split(speed[b, group(g), :]) for b in range(plan.bins) for g in range(plan.groups)
    ]
    pack(plan, rows_of, chunks, lambda i: i * plan.full, plan.core_rem)
    for k in range(plan.count):
        outs[k][...] = chunks[me ^ k]


def advect_kernel(plan, q1, south, above, east, north, *refs):
    outs = refs[: plan.count]
    ce, cn, fa, fb, nraw, chunks = refs[plan.count :]
    bins, groups, tiles = plan.bins, plan.groups, plan.tiles
    frame = groups + 4
    base = 2 * bins
    sub = sublanes(plan.lons)
    me = lax.axis_index("lev")
    last = lax.axis_index("lat") == lax.axis_size("lat") - 1

    for b in range(bins):
        for t in range(tiles):
            cut = slice(LANE * t, LANE * (t + 1))
            for buf in (fa, fb):
                buf[b, t, group(0), :] = jnp.zeros((SUB, LANE), F32)
                buf[b, t, group(frame + 1), :] = jnp.zeros((SUB, LANE), F32)
            for half in range(2):
                fa[b, t, group(1 + half), :] = south[group(2 * b + half), cut]
                fa[b, t, group(3 + groups + half), :] = above[group(2 * b + half), cut]
            fa[b, t, pl.ds(3 * SUB, plan.rows), :] = q1[b, :, cut]

    def put_east(g, value):
        for i, c in enumerate(coefficients(roll(value, 1, 1))):
            ce[i, group(g), :] = c

    put_east(0, roll(south[group(base + 2), :], 4, 0))
    put_east(1, south[group(base), :])
    loop(groups, lambda g: put_east(g + 2, east[group(g), :]))
    put_east(groups + 2, above[group(base), :])
    put_east(groups + 3, above[group(base + 2), :])

    nraw[group(0), :] = jnp.where(
        sub == 3, roll(south[group(0), :], 3, 0), south[group(base + 2), :]
    )
    nraw[group(1), :] = south[group(base + 1), :]
    nraw[pl.ds(2 * SUB, plan.rows - SUB), :] = north[pl.ds(0, plan.rows - SUB), :]
    closed = jnp.logical_and(last, sub == SUB - 1)
    nraw[group(groups + 1), :] = jnp.where(closed, 0.0, north[group(groups - 1), :])
    nraw[group(groups + 2), :] = above[group(base + 1), :]
    nraw[group(groups + 3), :] = roll(above[group(base + 2), :], 4, 0)

    def column(t):
        cut = pl.ds(pl.multiple_of(LANE * t, LANE), LANE)
        for i, c in enumerate(coefficients(roll(nraw[:, cut], 1, 0))):
            cn[i, :, cut] = c

    loop(tiles, column)

    rows = frame * SUB

    def meridional(src, dst):
        def body(t):
            cut = pl.ds(pl.multiple_of(LANE * t, LANE), LANE)
            co = [cn[i, :, cut] for i in range(3)]
            for b in range(bins):
                q, below2, below, beyond = (
                    src[b, t, pl.ds(SUB + d, rows), :] for d in (0, -2, -1, 1)
                )
                dst[b, t, pl.ds(SUB, rows), :] = swept(q, below2, below, beyond, co, 0)

        loop(tiles, body)

    def zonal_rows(src, dst, low, count):
        def body(i):
            g = i + low
            co = [ce[n, group(g), :] for n in range(3)]
            for b in range(bins):
                q = jnp.concatenate([src[b, t, group(g + 1), :] for t in range(tiles)], 1)
                q = zonal(q, co)
                for t in range(tiles):
                    dst[b, t, group(g + 1), :] = q[:, LANE * t : LANE * (t + 1)]

        loop(count, body)

    meridional(fa, fb)
    for step in range(1, HSUB):
        low = 1 if 3 * (step + 1) - 3 >= 8 else 0
        zonal_rows(fb, fa, low, frame - 2 * low)
        meridional(fa, fb)

    cores = [
        [fb[b, t, group(3 + g), :] for t in range(tiles)]
        for b in range(bins)
        for g in range(groups)
    ]
    pack(plan, cores, chunks, lambda i: i * plan.full, plan.core_rem)
    sub1 = sublanes(LANE)
    halos = [
        [
            jnp.where(sub1 < 4, fb[b, t, group(3 + groups), :], fb[b, t, group(2), :])
            for t in range(tiles)
        ]
        for b in range(bins)
    ]
    speeds = []
    for b in range(bins):
        at = base + 3 + b // 2
        v = jnp.where(sub < 4, above[group(at), :], south[group(at), :])
        if b % 2:
            v = jnp.where(sub < 4, roll(above[group(at), :], 4, 0), roll(south[group(at), :], 4, 0))
        speeds.append(split(v))
    halo_at = lambda i: plan.core + i * plan.full
    speed_at = lambda i: plan.field + i * plan.full
    if plan.shared:
        either = lambda i: halo_at(i) if i < bins else speed_at(i - bins)
        pack(plan, halos + speeds, chunks, either, plan.halo_rem)
    else:
        pack(plan, halos, chunks, halo_at, plan.halo_rem)
        pack(plan, speeds, chunks, speed_at, plan.speed_rem)
    for k in range(plan.count):
        outs[k][...] = chunks[me ^ k]


def settle_kernel(plan, *refs):
    n, bins = plan.count, plan.bins
    fields, speeds, deposit = refs[:n], refs[n : 2 * n], refs[2 * n]
    outs = refs[2 * n + 1 : 3 * n + 1]
    fld, fal, res, dep = refs[3 * n + 1 :]
    me = lax.axis_index("lev")
    for k in range(n):
        fld[me ^ k] = fields[k][...]
        fal[me ^ k, pl.ds(0, SUB * plan.core), :] = speeds[k][...]
    tiles = bins * plan.full
    for l in range(n):
        if tiles:
            fal[l, pl.ds(SUB * plan.core, SUB * tiles), :] = fld[
                l, pl.ds(SUB * plan.field, SUB * tiles), :
            ]
        for m in range(plan.field - plan.halo_rem):
            if plan.shared:
                v = roll(fld[l, group(plan.halo_rem), :], -bins * plan.rem, 1)
            else:
                v = fld[l, group(plan.speed_rem + m), :]
            fal[l, group(plan.halo_rem + m), :] = v

    size = next(c for c in (4, 2, 1) if plan.field % c == 0 and c * n <= 16)

    def body(i):
        rows = pl.ds(pl.multiple_of(i * SUB * size, SUB), SUB * size)
        q = [fld[l, rows, :] for l in range(n)]
        v = [fal[l, rows, :] for l in range(n)]
        total = None
        for _ in range(SETTLE_SUBSTEPS):
            inflow = None
            for l in range(n):
                flux = v[l] * (1.0 + 0.5 * jnp.tanh(q[l])) * q[l]
                q[l] = (q[l] if inflow is None else q[l] + inflow) - flux
                inflow = flux
            total = inflow if total is None else total + inflow
        for l in range(n):
            res[l, rows, :] = q[l]
        dep[rows, :] = total

    loop(plan.field // size, body)
    for k in range(n):
        outs[k][...] = res[me ^ k]
    for b in range(bins):
        for g in range(plan.groups):
            i = b * plan.groups + g
            for t in range(plan.full):
                deposit[b, group(g), LANE * t : LANE * (t + 1)] = dep[group(i * plan.full + t), :]
            if plan.rem:
                v = dep[group(plan.core_rem + i // plan.per), :]
                v = roll(v, -plan.rem * (i % plan.per), 1)
                deposit[b, group(g), LANE * plan.full :] = v[:, : plan.rem]


def close_kernel(plan, ce, cn, *refs):
    n, bins, groups, tiles = plan.count, plan.bins, plan.groups, plan.tiles
    ins, out = refs[:n], refs[n]
    parts, frame = refs[n + 1 :]
    me = lax.axis_index("lev")
    for k in range(n):
        parts[me ^ k] = ins[k][...]
    sub = sublanes(plan.lons)

    def swept_rows(b, at, index, rem_vector, slot, co):
        q = jnp.concatenate(unpack(plan, parts, index, rem_vector, slot), 1)
        for t, v in enumerate(split(zonal(q, co))):
            for a in at:
                frame[b, t, group(a), :] = v

    for g in range(groups):
        co = [ce[i, group(g + 2), :] for i in range(3)]
        for b in range(bins):
            i = b * groups + g
            swept_rows(
                b, (g + 2,), i * plan.full, plan.core_rem + i // plan.per, i % plan.per, co
            )
    co = [jnp.where(sub < 4, ce[i, group(groups + 2), :], ce[i, group(1), :]) for i in range(3)]
    for b in range(bins):
        swept_rows(
            b, (1, groups + 2), plan.core + b * plan.full,
            plan.halo_rem + b // plan.per, b % plan.per, co,
        )
    rows = (groups + 2) * SUB

    def body(t):
        cut = pl.ds(pl.multiple_of(LANE * t, LANE), LANE)
        co = [cn[i, pl.ds(SUB, rows), cut] for i in range(3)]
        for b in range(bins):
            q, below2, below, beyond = (
                frame[b, t, pl.ds(SUB + d, rows), :] for d in (0, -2, -1, 1)
            )
            out[b, :, cut] = swept(q, below2, below, beyond, co, 0)[SUB : SUB + plan.rows]

    loop(tiles, body)


def shape(*dims):
    return jax.ShapeDtypeStruct(dims, F32)


def call(kernel, plan, outs, scratch, name):
    return pl.pallas_call(
        functools.partial(kernel, plan), out_shape=outs, scratch_shapes=scratch, name=name
    )


def on_device(tracer, east, north, speed):
    bins, one, rows, lons = tracer.shape
    n, bands = lax.axis_size("lev"), lax.axis_size("lat")
    plan = Plan(bins, rows, lons, n)
    tracer, speed = tracer.reshape(bins, rows, lons), speed.reshape(bins, rows, lons)
    east, north = east.reshape(rows, lons), north.reshape(rows, lons)
    msg = SUB * plan.halo_groups
    frame = SUB * (plan.groups + 4)

    q1, up, down = call(
        start_kernel, plan, (shape(bins, rows, lons), shape(msg, lons), shape(msg, lons)), (),
        "start",
    )(tracer, east, north, speed)
    south = lax.ppermute(up, "lat", [(i, i + 1) for i in range(bands - 1)])
    above = lax.ppermute(down, "lat", [(i + 1, i) for i in range(bands - 1)])

    def exchanged(parts):
        return [parts[0]] + [
            lax.ppermute(parts[k], "lev", [(i, i ^ k) for i in range(n)]) for k in range(1, n)
        ]

    part = shape(SUB * plan.core, LANE)
    speeds = exchanged(
        call(
            speed_kernel, plan, (part,) * n, (pltpu.VMEM((n, SUB * plan.core, LANE), F32),), "speed"
        )(speed)
    )

    part = shape(SUB * plan.total, LANE)
    coef = shape(3, frame, lons)
    buf = pltpu.VMEM((bins, plan.tiles, frame + 2 * SUB, LANE), F32)
    *parts, ce, cn = call(
        advect_kernel, plan, (part,) * n + (coef, coef),
        (buf, buf, pltpu.VMEM((frame, lons), F32), pltpu.VMEM((n, SUB * plan.total, LANE), F32)),
        "advect",
    )(q1, south, above, east, north)
    fields = exchanged(parts)

    part = shape(SUB * plan.field, LANE)
    settled = pltpu.VMEM((n, SUB * plan.field, LANE), F32)
    deposit, *parts = call(
        settle_kernel, plan, (shape(bins, rows, plan.width),) + (part,) * n,
        (
            pltpu.VMEM((n, SUB * plan.total, LANE), F32), settled, settled,
            pltpu.VMEM((SUB * plan.field, LANE), F32),
        ),
        "settle",
    )(*fields, *speeds)
    parts = exchanged(parts)

    out = call(
        close_kernel, plan, shape(bins, rows, lons),
        (settled, pltpu.VMEM((bins, plan.tiles, frame, LANE), F32)), "close",
    )(ce, cn, *parts)
    return out.reshape(bins, one, rows, lons), deposit


def solution(mesh):
    in_specs = (
        P(None, "lev", "lat", None),
        P("lev", "lat", None),
        P("lev", "lat", None),
        P(None, "lev", "lat", None),
    )
    out_specs = (P(None, "lev", "lat", None), P(None, "lat", "lev"))
    return jax.shard_map(
        on_device, mesh=mesh, in_specs=in_specs, out_specs=out_specs, check_vma=False
    )
```

```python
import functools
import jax
import jax.numpy as jnp
from jax import lax
from jax.experimental import pallas as pl
from jax.experimental.pallas import tpu as pltpu
from jax.sharding import PartitionSpec as P

HSUB = 4
SETTLE_SUBSTEPS = 6
SUB = 8
LANE = 128
F32 = jnp.float32
VMEM_LIMIT = 16 << 20


def loop(count, body, unroll=1):
    def step(i, carry):
        body(i)
        return carry

    lax.fori_loop(0, count, step, 0, unroll=unroll)


def group(i):
    if isinstance(i, int):
        return pl.ds(SUB * i, SUB)
    return pl.ds(pl.multiple_of(SUB * i, SUB), SUB)


def roll(x, shift, axis):
    shift %= x.shape[axis]
    return pltpu.roll(x, shift, axis) if shift else x


def sublanes():
    return lax.broadcasted_iota(jnp.int32, (SUB, LANE), 0)


def lanes():
    return lax.broadcasted_iota(jnp.int32, (SUB, LANE), 1)


def coefficients(k):
    s = jnp.abs(k)
    r = 1.0 - s
    ks = k * s
    return k * (r * r), -(ks * r), ks * (3.0 - 2.0 * s)


def face(a, b, c, d):
    interp = (7.0 / 12.0) * (b + c) - (1.0 / 12.0) * (a + d)
    return jnp.minimum(jnp.maximum(interp, jnp.minimum(b, c)), jnp.maximum(b, c))


def flux(co, f, f_below, f_above, below, q):
    al, be, ga = co
    up = al >= 0
    return al * f + be * jnp.where(up, f_below, f_above) + ga * jnp.where(up, below, q)


def zonal(q, co):
    count = len(q)
    e = [roll(q[-2], 1, 1), roll(q[-1], 1, 1), *q, roll(q[0], -1, 1)]
    f = [face(*e[p : p + 4]) for p in range(count)]
    f = [roll(f[-1], 1, 1), *f, roll(f[0], -1, 1)]
    w = [flux(co[p], f[p + 1], f[p], f[p + 2], e[p + 1], q[p]) for p in range(count)]
    w.append(roll(w[0], -1, 1))
    return [q[p] - (w[p + 1] - w[p]) for p in range(count)]


def meridional(q, below2, below, above, co):
    f = face(below2, below, q, above)
    w = flux(co, f, roll(f, 1, 0), roll(f, -1, 0), below, q)
    return q - (roll(w, -1, 0) - w)


class Plan:
    def __init__(self, bins, rows, lons, count):
        self.bins, self.rows, self.lons, self.count = bins, rows, lons, count
        self.groups, self.tiles = rows // SUB, lons // LANE
        self.width = LANE // count
        self.vectors = -(-(self.groups + 2) // count)
        self.message = bins * self.tiles * self.vectors
        self.halo_groups = 2 * bins + 3 + (bins + 1) // 2

    def at(self, b, p, v):
        return group((b * self.tiles + p) * self.vectors + v)


def interleave(plan, src, turned, put):
    rows = src.shape[0]
    for t in range(plan.tiles):
        turned[pl.ds(LANE * t, LANE), :rows] = src[:, LANE * t : LANE * (t + 1)].T
    for p in range(plan.tiles):
        put(p, turned[pl.ds(p, LANE, stride=plan.tiles), :].T[:rows])


def scatter(plan, xs):
    out = []
    for j in range(plan.count):
        y = roll(xs[0], -j * plan.width, 1)
        for s in range(1, len(xs)):
            y = jnp.where(lanes() < s * plan.width, y, roll(xs[s], (s - j) * plan.width, 1))
        out.append(y)
    return out


def gather(plan, ys, slot):
    x = roll(ys[0], -slot * plan.width, 1)
    for j in range(1, plan.count):
        x = jnp.where(lanes() < j * plan.width, x, roll(ys[j], (j - slot) * plan.width, 1))
    return x


def pack(plan, chunks, b, p, xs):
    for v in range(0, len(xs), plan.count):
        for j, y in enumerate(scatter(plan, xs[v : v + plan.count])):
            chunks[j, plan.at(b, p, v // plan.count), :] = y


def start_kernel(
    plan, tracer, east, north, speed, q1, ce, ns, up, down, x0, x1, turned, s0, s1, sem
):
    bins, rows, tiles, top = plan.bins, plan.rows, plan.tiles, plan.groups - 1
    moves = [(tracer.at[b], x0.at[pl.ds(b * rows, rows)]) for b in range(bins)]
    moves.append((east, x1.at[pl.ds(0, rows)]))
    moves.append((north, x1.at[pl.ds(rows, rows)]))
    edge = 2 * plan.groups
    for b in range(bins):
        for half, g in enumerate((0, top)):
            moves.append((speed.at[b, group(g)], x1.at[group(edge + 2 * b + half)]))
    copies = [pltpu.make_async_copy(*m, sem.at[i]) for i, m in enumerate(moves)]
    for c in copies:
        c.start()
    for c in copies[:bins]:
        c.wait()

    def put0(p, v):
        s0[p] = v

    def put1(p, v):
        s1[p] = v

    interleave(plan, x0, turned.at[0], put0)
    for c in copies[bins:]:
        c.wait()
    interleave(plan, x1, turned.at[1], put1)

    def body(g):
        k = [s1[p, group(g), :] for p in range(tiles)]
        co = [coefficients(c) for c in [roll(k[-1], 1, 1), *k[:-1]]]
        for p in range(tiles):
            for i in range(3):
                ce[i, p, group(g), :] = co[p][i]
        for b in range(bins):
            q = zonal([s0[p, group(b * plan.groups + g), :] for p in range(tiles)], co)
            for p in range(tiles):
                q1[b, p, group(g), :] = q[p]

    loop(plan.groups, body, 2)
    sub = sublanes()
    base = 2 * bins

    def message(p):
        ns[p] = s1[p, pl.ds(rows, rows), :]
        east_at = lambda g: s1[p, group(g), :]
        north_at = lambda g: s1[p, group(plan.groups + g), :]
        speed_at = lambda b, half: s1[p, group(edge + 2 * b + half), :]
        for b in range(bins):
            for half in range(2):
                v = q1[b, p, group(top - 1 + half), :]
                if b == 0 and half == 0:
                    v = jnp.where(sub == 0, roll(north_at(top - 1), -3, 0), v)
                up[p, group(2 * b + half), :] = v
                down[p, group(2 * b + half), :] = q1[b, p, group(half), :]
        up[p, group(base), :] = east_at(top)
        up[p, group(base + 1), :] = north_at(top)
        up[p, group(base + 2), :] = jnp.where(
            sub < 4, roll(east_at(top - 1), 4, 0), north_at(top - 1)
        )
        down[p, group(base), :] = east_at(0)
        down[p, group(base + 1), :] = north_at(0)
        down[p, group(base + 2), :] = jnp.where(sub < 4, east_at(1), roll(north_at(1), 4, 0))
        for h in range((bins + 1) // 2):
            a, b = 2 * h, min(2 * h + 1, bins - 1)
            up[p, group(base + 3 + h), :] = jnp.where(
                sub < 4, roll(speed_at(b, 1), 4, 0), speed_at(a, 1)
            )
            down[p, group(base + 3 + h), :] = jnp.where(
                sub < 4, speed_at(a, 0), roll(speed_at(b, 0), 4, 0)
            )

    loop(tiles, message)


def speed_kernel(plan, speed, *refs):
    outs, (turned, s, chunks) = refs[:-3], refs[-3:]
    me = lax.axis_index("lev")

    def put(p, v):
        s[p] = v

    interleave(plan, speed, turned, put)

    def body(p):
        for b in range(plan.bins):
            xs = [s[p, group(b * plan.groups + g), :] for g in range(plan.groups)]
            pack(plan, chunks, b, p, xs)

    loop(plan.tiles, body)
    for k in range(plan.count):
        outs[k][...] = chunks[me ^ k]


def advect_kernel(plan, q1, ce, ns, south, above, *refs):
    outs = refs[: plan.count]
    ceh, cn, fa, fb, nraw, halo, chunks = refs[plan.count :]
    bins, groups, tiles = plan.bins, plan.groups, plan.tiles
    frame = groups + 4
    rows = frame * SUB
    base = 2 * bins
    sub = sublanes()
    me = lax.axis_index("lev")
    last = lax.axis_index("lat") == lax.axis_size("lat") - 1
    closed = jnp.logical_and(last, sub == SUB - 1)

    def fill(p):
        for b in range(bins):
            for buf in (fa, fb):
                buf[b, p, group(0), :] = jnp.zeros((SUB, LANE), F32)
                buf[b, p, group(frame + 1), :] = jnp.zeros((SUB, LANE), F32)
            for half in range(2):
                fa[b, p, group(1 + half), :] = south[p, group(2 * b + half), :]
                fa[b, p, group(3 + groups + half), :] = above[p, group(2 * b + half), :]
            fa[b, p, pl.ds(3 * SUB, plan.rows), :] = q1[b, p]
        nraw[group(0), :] = jnp.where(
            sub == 3, roll(south[p, group(0), :], 3, 0), south[p, group(base + 2), :]
        )
        nraw[group(1), :] = south[p, group(base + 1), :]
        nraw[pl.ds(2 * SUB, plan.rows - SUB), :] = ns[p, pl.ds(0, plan.rows - SUB), :]
        nraw[group(groups + 1), :] = jnp.where(closed, 0.0, ns[p, group(groups - 1), :])
        nraw[group(groups + 2), :] = above[p, group(base + 1), :]
        nraw[group(groups + 3), :] = roll(above[p, group(base + 2), :], 4, 0)
        for i, c in enumerate(coefficients(roll(nraw[...], 1, 0))):
            cn[i, p] = c

    loop(tiles, fill)
    courants = (
        [roll(south[p, group(base + 2), :], 4, 0) for p in range(tiles)],
        [south[p, group(base), :] for p in range(tiles)],
        [above[p, group(base), :] for p in range(tiles)],
        [above[p, group(base + 2), :] for p in range(tiles)],
    )
    for g, k in enumerate(courants):
        for p, c in enumerate([roll(k[-1], 1, 1), *k[:-1]]):
            for i, v in enumerate(coefficients(c)):
                halo[i, p, group(g), :] = v
    for p in range(tiles):
        for i in range(3):
            ceh[i, p] = jnp.where(sub < 4, halo[i, p, group(2), :], halo[i, p, group(1), :])

    def meridional_sweep(src, dst):
        def body(p):
            co = [cn[i, p] for i in range(3)]
            for b in range(bins):
                q, below2, below, beyond = (
                    src[b, p, pl.ds(SUB + d, rows), :] for d in (0, -2, -1, 1)
                )
                dst[b, p, pl.ds(SUB, rows), :] = meridional(q, below2, below, beyond, co)

        loop(tiles, body)

    def zonal_sweep(src, dst, low):
        def row_group(g, table, index):
            co = [[table[i, p, group(index), :] for i in range(3)] for p in range(tiles)]
            for b in range(bins):
                q = zonal([src[b, p, group(g), :] for p in range(tiles)], co)
                for p in range(tiles):
                    dst[b, p, group(g), :] = q[p]

        loop(groups, lambda i: row_group(3 + i, ce, i), 2)
        for g in range(low, 4 - low):
            row_group(1 + g if g < 2 else 1 + groups + g, halo, g)

    meridional_sweep(fa, fb)
    for step in range(1, HSUB):
        zonal_sweep(fb, fa, 1 if 3 * step >= 8 else 0)
        meridional_sweep(fa, fb)

    def columns(p):
        for b in range(bins):
            xs = [fb[b, p, group(3 + g), :] for g in range(groups)]
            xs.append(jnp.where(sub < 4, fb[b, p, group(3 + groups), :], fb[b, p, group(2), :]))
            at = group(base + 3 + b // 2)
            parts = above[p, at, :], south[p, at, :]
            if b % 2:
                parts = [roll(v, 4, 0) for v in parts]
            xs.append(jnp.where(sub < 4, *parts))
            pack(plan, chunks, b, p, xs)

    loop(tiles, columns)
    for k in range(plan.count):
        outs[k][...] = chunks[me ^ k]


def settle_kernel(plan, *refs):
    n, groups = plan.count, plan.groups
    fields, speeds, deposited = refs[:n], refs[n : 2 * n], refs[2 * n]
    outs = refs[2 * n + 1 : 3 * n + 1]
    fld, fal, res = refs[3 * n + 1 :]
    me = lax.axis_index("lev")
    for k in range(n):
        fld[me ^ k] = fields[k][...]
        fal[me ^ k] = speeds[k][...]
    halo, halo_slot = divmod(groups, n)
    speed, speed_slot = divmod(groups + 1, n)
    low, high = halo_slot * plan.width, (halo_slot + 1) * plan.width
    here = jnp.logical_and(lanes() >= low, lanes() < high)

    def body(i):
        for vector in range(plan.vectors):
            rows = group(i * plan.vectors + vector)
            q = [fld[l, rows, :] for l in range(n)]
            v = [fal[l, rows, :] for l in range(n)]
            if vector == halo:
                own = group(i * plan.vectors + speed)
                turn = (halo_slot - speed_slot) * plan.width
                v = [jnp.where(here, roll(fld[l, own, :], turn, 1), v[l]) for l in range(n)]
            h = [0.5 * x for x in v]
            total = None
            for _ in range(SETTLE_SUBSTEPS):
                inflow = None
                for l in range(n):
                    down = (v[l] + h[l] * jnp.tanh(q[l])) * q[l]
                    q[l] = (q[l] if inflow is None else q[l] + inflow) - down
                    inflow = down
                total = inflow if total is None else total + inflow
            for l in range(n):
                res[l, rows, :] = q[l]
            deposited[rows, :] = total

    loop(plan.message // plan.vectors, body, 2)
    for k in range(n):
        outs[k][...] = res[me ^ k]


def deposit_kernel(plan, deposited, deposit, side, turned):
    n, groups, tiles, width = plan.count, plan.groups, plan.tiles, plan.width
    rows = plan.bins * plan.rows
    for first in range(0, tiles, n):
        held = range(first, min(first + n, tiles))
        for b in range(plan.bins):
            for g in range(groups):
                y = None
                for s, p in enumerate(held):
                    x = deposited[plan.at(b, p, g // n), :]
                    x = roll(x, (s - g % n) * width, 1)
                    y = x if y is None else jnp.where(lanes() < s * width, y, x)
                side[group(b * groups + g), :] = y
        x = side[...].T
        for s, p in enumerate(held):
            turned[pl.ds(p, width, stride=tiles), :rows] = x[s * width : (s + 1) * width]
    lons = tiles * width
    for t in range(-(-lons // LANE)):
        x = turned[pl.ds(LANE * t, LANE), :].T[:rows]
        end = min(LANE * (t + 1), lons)
        for b in range(plan.bins):
            deposit[b, :, LANE * t : end] = x[b * plan.rows : (b + 1) * plan.rows, : end - LANE * t]


def close_kernel(plan, ce, ceh, cn, *refs):
    n, bins, groups, tiles = plan.count, plan.bins, plan.groups, plan.tiles
    ins, out = refs[:n], refs[n]
    parts, spread, frame, done, turned = refs[n + 1 :]
    me = lax.axis_index("lev")
    for k in range(n):
        parts[me ^ k] = ins[k][...]

    def place(p):
        for b in range(bins):
            for g in range(groups + 1):
                ys = [parts[j, plan.at(b, p, g // n), :] for j in range(n)]
                spread[b, p, group(g), :] = gather(plan, ys, g % n)

    loop(tiles, place)

    def row_group(g, table, index, targets):
        co = [[table[i, p, group(index), :] for i in range(3)] for p in range(tiles)]
        for b in range(bins):
            q = zonal([spread[b, p, group(g), :] for p in range(tiles)], co)
            for p in range(tiles):
                for a in targets:
                    frame[b, p, group(a), :] = q[p]

    loop(groups, lambda g: row_group(g, ce, g, (g + 2,)), 2)
    row_group(groups, ceh, 0, (1, groups + 2))
    rows = plan.rows + 2 * SUB

    def body(p):
        co = [cn[i, p, pl.ds(SUB, rows), :] for i in range(3)]
        for b in range(bins):
            q, below2, below, beyond = (
                frame[b, p, pl.ds(SUB + d, rows), :] for d in (0, -2, -1, 1)
            )
            q = meridional(q, below2, below, beyond, co)
            done[p, pl.ds(b * plan.rows, plan.rows), :] = q[SUB : SUB + plan.rows]

    loop(tiles, body)
    rows = bins * plan.rows
    for p in range(tiles):
        turned[pl.ds(p, LANE, stride=tiles), :rows] = done[p].T
    for t in range(tiles):
        x = turned[pl.ds(LANE * t, LANE), :].T
        for b in range(bins):
            out[b, :, LANE * t : LANE * (t + 1)] = x[b * plan.rows : (b + 1) * plan.rows]


def shape(*dims):
    return jax.ShapeDtypeStruct(dims, F32)


def call(kernel, plan, outs, scratch, name, space=pltpu.VMEM):
    held = pl.BlockSpec(memory_space=pltpu.VMEM)
    return lambda *args: pl.pallas_call(
        functools.partial(kernel, plan), out_shape=outs, scratch_shapes=scratch, name=name,
        in_specs=[pl.BlockSpec(memory_space=space)] * len(args),
        out_specs=jax.tree.map(lambda _: held, outs),
        compiler_params=pltpu.CompilerParams(vmem_limit_bytes=VMEM_LIMIT),
    )(*args)


def vmem(*dims):
    return pltpu.VMEM(dims, F32)


def on_device(tracer, east, north, speed):
    bins, one, rows, lons = tracer.shape
    n, bands = lax.axis_size("lev"), lax.axis_size("lat")
    plan = Plan(bins, rows, lons, n)
    tiles, frame = plan.tiles, rows + 4 * SUB
    tracer, speed = tracer.reshape(bins, rows, lons), speed.reshape(bins, rows, lons)
    east, north = east.reshape(rows, lons), north.reshape(rows, lons)

    band = shape(tiles, SUB * plan.halo_groups, LANE)
    edge = 2 * rows + 2 * SUB * bins
    q1, ce, ns, up, down = call(
        start_kernel, plan,
        (shape(bins, tiles, rows, LANE), shape(3, tiles, rows, LANE), shape(tiles, rows, LANE), band, band),
        (
            vmem(bins * rows, lons), vmem(edge, lons), vmem(2, lons, LANE),
            vmem(tiles, bins * rows, LANE), vmem(tiles, edge, LANE),
            pltpu.SemaphoreType.DMA((3 * bins + 2,)),
        ),
        "start", pl.ANY,
    )(tracer, east, north, speed)
    south = lax.ppermute(up, "lat", [(i, i + 1) for i in range(bands - 1)])
    above = lax.ppermute(down, "lat", [(i + 1, i) for i in range(bands - 1)])

    def exchanged(parts):
        return [parts[0]] + [
            lax.ppermute(parts[k], "lev", [(i, i ^ k) for i in range(n)]) for k in range(1, n)
        ]

    part = shape(SUB * plan.message, LANE)
    every = vmem(n, SUB * plan.message, LANE)
    speeds = exchanged(
        call(
            speed_kernel, plan, (part,) * n,
            (vmem(lons, LANE), vmem(tiles, bins * rows, LANE), every), "speed",
        )(speed.reshape(bins * rows, lons))
    )

    buf = vmem(bins, tiles, frame + 2 * SUB, LANE)
    *parts, ceh, cn = call(
        advect_kernel, plan,
        (part,) * n + (shape(3, tiles, SUB, LANE), shape(3, tiles, frame, LANE)),
        (buf, buf, vmem(frame, LANE), vmem(3, tiles, 4 * SUB, LANE), every), "advect",
    )(q1, ce, ns, south, above)
    fields = exchanged(parts)

    deposited, *parts = call(
        settle_kernel, plan, (part,) + (part,) * n, (every, every, every), "settle"
    )(*fields, *speeds)
    parts = exchanged(parts)
    local = tiles * plan.width
    deposit = call(
        deposit_kernel, plan, shape(bins, rows, local),
        (vmem(bins * rows, LANE), vmem(-(-local // LANE) * LANE, LANE)), "deposit",
    )(deposited)

    out = call(
        close_kernel, plan, shape(bins, rows, lons),
        (
            every, vmem(bins, tiles, rows + SUB, LANE), vmem(bins, tiles, frame, LANE),
            vmem(tiles, bins * rows, LANE), vmem(lons, LANE),
        ),
        "close",
    )(ce, ceh, cn, *parts)
    return out.reshape(bins, one, rows, lons), deposit


def solution(mesh):
    in_specs = (
        P(None, "lev", "lat", None),
        P("lev", "lat", None),
        P("lev", "lat", None),
        P(None, "lev", "lat", None),
    )
    out_specs = (P(None, "lev", "lat", None), P(None, "lat", "lev"))
    return jax.shard_map(
        on_device, mesh=mesh, in_specs=in_specs, out_specs=out_specs, check_vma=False
    )
```

```python
import functools
import jax
import jax.numpy as jnp
from jax import lax
from jax.experimental import pallas as pl
from jax.experimental.pallas import tpu as pltpu
from jax.sharding import PartitionSpec as P

HSUB = 4
SETTLE_SUBSTEPS = 6
SUB = 8
LANE = 128
F32 = jnp.float32
VMEM_LIMIT = 16 << 20


def loop(count, body, unroll=1):
    def step(i, carry):
        body(i)
        return carry

    lax.fori_loop(0, count, step, 0, unroll=unroll)


def group(i):
    if isinstance(i, int):
        return pl.ds(SUB * i, SUB)
    return pl.ds(pl.multiple_of(SUB * i, SUB), SUB)


def roll(x, shift, axis):
    shift %= x.shape[axis]
    return pltpu.roll(x, shift, axis) if shift else x


def sublanes():
    return lax.broadcasted_iota(jnp.int32, (SUB, LANE), 0)


def lanes():
    return lax.broadcasted_iota(jnp.int32, (SUB, LANE), 1)


def coefficients(k):
    s = jnp.abs(k)
    r = 1.0 - s
    ks = k * s
    return k * (r * r), -(ks * r), ks * (3.0 - 2.0 * s)


def face(a, b, c, d):
    interp = (7.0 / 12.0) * (b + c) - (1.0 / 12.0) * (a + d)
    return jnp.minimum(jnp.maximum(interp, jnp.minimum(b, c)), jnp.maximum(b, c))


def flux(co, f, f_below, f_above, below, q):
    al, be, ga = co
    up = al >= 0
    return al * f + be * jnp.where(up, f_below, f_above) + ga * jnp.where(up, below, q)


def zonal(q, co):
    count = len(q)
    e = [roll(q[-2], 1, 1), roll(q[-1], 1, 1), *q, roll(q[0], -1, 1)]
    f = [face(*e[p : p + 4]) for p in range(count)]
    f = [roll(f[-1], 1, 1), *f, roll(f[0], -1, 1)]
    w = [flux(co[p], f[p + 1], f[p], f[p + 2], e[p + 1], q[p]) for p in range(count)]
    w.append(roll(w[0], -1, 1))
    return [q[p] - (w[p + 1] - w[p]) for p in range(count)]


def meridional(q, below2, below, above, co):
    f = face(below2, below, q, above)
    w = flux(co, f, roll(f, 1, 0), roll(f, -1, 0), below, q)
    return q - (roll(w, -1, 0) - w)


class Plan:
    def __init__(self, bins, rows, lons, count):
        self.bins, self.rows, self.lons, self.count = bins, rows, lons, count
        self.groups, self.tiles = rows // SUB, lons // LANE
        self.width = LANE // count
        self.vectors = -(-(self.groups + 2) // count)
        self.message = bins * self.tiles * self.vectors
        self.halo_groups = 2 * bins + 3 + (bins + 1) // 2

    def at(self, b, p, v):
        return group((b * self.tiles + p) * self.vectors + v)


def interleave(plan, src, turned, put):
    rows = src.shape[0]
    for t in range(plan.tiles):
        turned[pl.ds(LANE * t, LANE), :rows] = src[:, LANE * t : LANE * (t + 1)].T
    for p in range(plan.tiles):
        put(p, turned[pl.ds(p, LANE, stride=plan.tiles), :].T[:rows])


def scatter(plan, xs):
    out = []
    for j in range(plan.count):
        y = roll(xs[0], -j * plan.width, 1)
        for s in range(1, len(xs)):
            y = jnp.where(lanes() < s * plan.width, y, roll(xs[s], (s - j) * plan.width, 1))
        out.append(y)
    return out


def gather(plan, ys, slot):
    x = roll(ys[0], -slot * plan.width, 1)
    for j in range(1, plan.count):
        x = jnp.where(lanes() < j * plan.width, x, roll(ys[j], (j - slot) * plan.width, 1))
    return x


def pack(plan, chunks, b, p, xs):
    for v in range(0, len(xs), plan.count):
        for j, y in enumerate(scatter(plan, xs[v : v + plan.count])):
            chunks[j, plan.at(b, p, v // plan.count), :] = y


def start_kernel(
    plan, tracer, east, north, speed, q1, ce, ns, up, down, x0, x1, turned, s0, s1, sem
):
    bins, rows, tiles, top = plan.bins, plan.rows, plan.tiles, plan.groups - 1
    moves = [(tracer.at[b], x0.at[pl.ds(b * rows, rows)]) for b in range(bins)]
    moves.append((east, x1.at[pl.ds(0, rows)]))
    moves.append((north, x1.at[pl.ds(rows, rows)]))
    edge = 2 * plan.groups
    for b in range(bins):
        for half, g in enumerate((0, top)):
            moves.append((speed.at[b, group(g)], x1.at[group(edge + 2 * b + half)]))
    copies = [pltpu.make_async_copy(*m, sem.at[i]) for i, m in enumerate(moves)]
    for c in copies:
        c.start()
    for c in copies[:bins]:
        c.wait()

    def put0(p, v):
        s0[p] = v

    def put1(p, v):
        s1[p] = v

    interleave(plan, x0, turned.at[0], put0)
    for c in copies[bins:]:
        c.wait()
    interleave(plan, x1, turned.at[1], put1)

    def body(g):
        k = [s1[p, group(g), :] for p in range(tiles)]
        co = [coefficients(c) for c in [roll(k[-1], 1, 1), *k[:-1]]]
        for p in range(tiles):
            for i in range(3):
                ce[i, p, group(g), :] = co[p][i]
        for b in range(bins):
            q = zonal([s0[p, group(b * plan.groups + g), :] for p in range(tiles)], co)
            for p in range(tiles):
                q1[b, p, group(g), :] = q[p]

    loop(plan.groups, body, 2)
    sub = sublanes()
    base = 2 * bins

    def message(p):
        ns[p] = s1[p, pl.ds(rows, rows), :]
        east_at = lambda g: s1[p, group(g), :]
        north_at = lambda g: s1[p, group(plan.groups + g), :]
        speed_at = lambda b, half: s1[p, group(edge + 2 * b + half), :]
        for b in range(bins):
            for half in range(2):
                v = q1[b, p, group(top - 1 + half), :]
                if b == 0 and half == 0:
                    v = jnp.where(sub == 0, roll(north_at(top - 1), -3, 0), v)
                up[p, group(2 * b + half), :] = v
                down[p, group(2 * b + half), :] = q1[b, p, group(half), :]
        up[p, group(base), :] = east_at(top)
        up[p, group(base + 1), :] = north_at(top)
        up[p, group(base + 2), :] = jnp.where(
            sub < 4, roll(east_at(top - 1), 4, 0), north_at(top - 1)
        )
        down[p, group(base), :] = east_at(0)
        down[p, group(base + 1), :] = north_at(0)
        down[p, group(base + 2), :] = jnp.where(sub < 4, east_at(1), roll(north_at(1), 4, 0))
        for h in range((bins + 1) // 2):
            a, b = 2 * h, min(2 * h + 1, bins - 1)
            up[p, group(base + 3 + h), :] = jnp.where(
                sub < 4, roll(speed_at(b, 1), 4, 0), speed_at(a, 1)
            )
            down[p, group(base + 3 + h), :] = jnp.where(
                sub < 4, speed_at(a, 0), roll(speed_at(b, 0), 4, 0)
            )

    loop(tiles, message)


def speed_kernel(plan, speed, *refs):
    outs, (turned, s, chunks) = refs[:-3], refs[-3:]
    me = lax.axis_index("lev")

    def put(p, v):
        s[p] = v

    interleave(plan, speed, turned, put)

    def body(p):
        for b in range(plan.bins):
            xs = [s[p, group(b * plan.groups + g), :] for g in range(plan.groups)]
            pack(plan, chunks, b, p, xs)

    loop(plan.tiles, body)
    for k in range(plan.count):
        outs[k][...] = chunks[me ^ k]


def advect_kernel(plan, q1, ce, ns, south, above, *refs):
    outs = refs[: plan.count]
    ceh, cn, fa, fb, nraw, halo, chunks = refs[plan.count :]
    bins, groups, tiles = plan.bins, plan.groups, plan.tiles
    frame = groups + 4
    rows = frame * SUB
    base = 2 * bins
    sub = sublanes()
    me = lax.axis_index("lev")
    last = lax.axis_index("lat") == lax.axis_size("lat") - 1
    closed = jnp.logical_and(last, sub == SUB - 1)

    def fill(p):
        for b in range(bins):
            for buf in (fa, fb):
                buf[b, p, group(0), :] = jnp.zeros((SUB, LANE), F32)
                buf[b, p, group(frame + 1), :] = jnp.zeros((SUB, LANE), F32)
            for half in range(2):
                fa[b, p, group(1 + half), :] = south[p, group(2 * b + half), :]
                fa[b, p, group(3 + groups + half), :] = above[p, group(2 * b + half), :]
            fa[b, p, pl.ds(3 * SUB, plan.rows), :] = q1[b, p]
        nraw[group(0), :] = jnp.where(
            sub == 3, roll(south[p, group(0), :], 3, 0), south[p, group(base + 2), :]
        )
        nraw[group(1), :] = south[p, group(base + 1), :]
        nraw[pl.ds(2 * SUB, plan.rows - SUB), :] = ns[p, pl.ds(0, plan.rows - SUB), :]
        nraw[group(groups + 1), :] = jnp.where(closed, 0.0, ns[p, group(groups - 1), :])
        nraw[group(groups + 2), :] = above[p, group(base + 1), :]
        nraw[group(groups + 3), :] = roll(above[p, group(base + 2), :], 4, 0)
        for i, c in enumerate(coefficients(roll(nraw[...], 1, 0))):
            cn[i, p] = c

    loop(tiles, fill)
    courants = (
        [roll(south[p, group(base + 2), :], 4, 0) for p in range(tiles)],
        [south[p, group(base), :] for p in range(tiles)],
        [above[p, group(base), :] for p in range(tiles)],
        [above[p, group(base + 2), :] for p in range(tiles)],
    )
    for g, k in enumerate(courants):
        for p, c in enumerate([roll(k[-1], 1, 1), *k[:-1]]):
            for i, v in enumerate(coefficients(c)):
                halo[i, p, group(g), :] = v
    for p in range(tiles):
        for i in range(3):
            ceh[i, p] = jnp.where(sub < 4, halo[i, p, group(2), :], halo[i, p, group(1), :])

    def meridional_sweep(src, dst):
        def body(p):
            co = [cn[i, p] for i in range(3)]
            for b in range(bins):
                q, below2, below, beyond = (
                    src[b, p, pl.ds(SUB + d, rows), :] for d in (0, -2, -1, 1)
                )
                dst[b, p, pl.ds(SUB, rows), :] = meridional(q, below2, below, beyond, co)

        loop(tiles, body)

    def zonal_sweep(src, dst, low):
        def row_group(g, table, index):
            co = [[table[i, p, group(index), :] for i in range(3)] for p in range(tiles)]
            for b in range(bins):
                q = zonal([src[b, p, group(g), :] for p in range(tiles)], co)
                for p in range(tiles):
                    dst[b, p, group(g), :] = q[p]

        loop(groups, lambda i: row_group(3 + i, ce, i), 2)
        for g in range(low, 4 - low):
            row_group(1 + g if g < 2 else 1 + groups + g, halo, g)

    meridional_sweep(fa, fb)
    for step in range(1, HSUB):
        zonal_sweep(fb, fa, 1 if 3 * step >= 8 else 0)
        meridional_sweep(fa, fb)

    def columns(p):
        for b in range(bins):
            xs = [fb[b, p, group(3 + g), :] for g in range(groups)]
            xs.append(jnp.where(sub < 4, fb[b, p, group(3 + groups), :], fb[b, p, group(2), :]))
            at = group(base + 3 + b // 2)
            parts = above[p, at, :], south[p, at, :]
            if b % 2:
                parts = [roll(v, 4, 0) for v in parts]
            xs.append(jnp.where(sub < 4, *parts))
            pack(plan, chunks, b, p, xs)

    loop(tiles, columns)
    for k in range(plan.count):
        outs[k][...] = chunks[me ^ k]


def settle_kernel(plan, *refs):
    n, groups = plan.count, plan.groups
    fields, speeds, deposited = refs[:n], refs[n : 2 * n], refs[2 * n]
    outs = refs[2 * n + 1 : 3 * n + 1]
    fld, fal, res = refs[3 * n + 1 :]
    me = lax.axis_index("lev")
    for k in range(n):
        fld[me ^ k] = fields[k][...]
        fal[me ^ k] = speeds[k][...]
    halo, halo_slot = divmod(groups, n)
    speed, speed_slot = divmod(groups + 1, n)
    low, high = halo_slot * plan.width, (halo_slot + 1) * plan.width
    here = jnp.logical_and(lanes() >= low, lanes() < high)

    def body(i):
        for vector in range(plan.vectors):
            rows = group(i * plan.vectors + vector)
            q = [fld[l, rows, :] for l in range(n)]
            v = [fal[l, rows, :] for l in range(n)]
            if vector == halo:
                own = group(i * plan.vectors + speed)
                turn = (halo_slot - speed_slot) * plan.width
                v = [jnp.where(here, roll(fld[l, own, :], turn, 1), v[l]) for l in range(n)]
            h = [0.5 * x for x in v]
            total = None
            for _ in range(SETTLE_SUBSTEPS):
                inflow = None
                for l in range(n):
                    down = (v[l] + h[l] * jnp.tanh(q[l])) * q[l]
                    q[l] = (q[l] if inflow is None else q[l] + inflow) - down
                    inflow = down
                total = inflow if total is None else total + inflow
            for l in range(n):
                res[l, rows, :] = q[l]
            deposited[rows, :] = total

    loop(plan.message // plan.vectors, body, 2)
    for k in range(n):
        outs[k][...] = res[me ^ k]


def deposit_kernel(plan, deposited, deposit, side, turned):
    n, groups, tiles, width = plan.count, plan.groups, plan.tiles, plan.width
    rows = plan.bins * plan.rows
    for first in range(0, tiles, n):
        held = range(first, min(first + n, tiles))
        for b in range(plan.bins):
            for g in range(groups):
                y = None
                for s, p in enumerate(held):
                    x = deposited[plan.at(b, p, g // n), :]
                    x = roll(x, (s - g % n) * width, 1)
                    y = x if y is None else jnp.where(lanes() < s * width, y, x)
                side[group(b * groups + g), :] = y
        x = side[...].T
        for s, p in enumerate(held):
            turned[pl.ds(p, width, stride=tiles), :rows] = x[s * width : (s + 1) * width]
    lons = tiles * width
    for t in range(-(-lons // LANE)):
        x = turned[pl.ds(LANE * t, LANE), :].T[:rows]
        end = min(LANE * (t + 1), lons)
        for b in range(plan.bins):
            deposit[b, :, LANE * t : end] = x[b * plan.rows : (b + 1) * plan.rows, : end - LANE * t]


def close_kernel(plan, ce, ceh, cn, *refs):
    n, bins, groups, tiles = plan.count, plan.bins, plan.groups, plan.tiles
    ins, out = refs[:n], refs[n]
    parts, spread, frame, done, turned = refs[n + 1 :]
    me = lax.axis_index("lev")
    for k in range(n):
        parts[me ^ k] = ins[k][...]

    def place(p):
        for b in range(bins):
            for g in range(groups + 1):
                ys = [parts[j, plan.at(b, p, g // n), :] for j in range(n)]
                spread[b, p, group(g), :] = gather(plan, ys, g % n)

    loop(tiles, place)

    def row_group(g, table, index, targets):
        co = [[table[i, p, group(index), :] for i in range(3)] for p in range(tiles)]
        for b in range(bins):
            q = zonal([spread[b, p, group(g), :] for p in range(tiles)], co)
            for p in range(tiles):
                for a in targets:
                    frame[b, p, group(a), :] = q[p]

    loop(groups, lambda g: row_group(g, ce, g, (g + 2,)), 2)
    row_group(groups, ceh, 0, (1, groups + 2))
    rows = plan.rows + 2 * SUB

    def body(p):
        co = [cn[i, p, pl.ds(SUB, rows), :] for i in range(3)]
        for b in range(bins):
            q, below2, below, beyond = (
                frame[b, p, pl.ds(SUB + d, rows), :] for d in (0, -2, -1, 1)
            )
            q = meridional(q, below2, below, beyond, co)
            done[p, pl.ds(b * plan.rows, plan.rows), :] = q[SUB : SUB + plan.rows]

    loop(tiles, body)
    rows = bins * plan.rows
    for p in range(tiles):
        turned[pl.ds(p, LANE, stride=tiles), :rows] = done[p].T
    for t in range(tiles):
        x = turned[pl.ds(LANE * t, LANE), :].T
        for b in range(bins):
            out[b, :, LANE * t : LANE * (t + 1)] = x[b * plan.rows : (b + 1) * plan.rows]


def shape(*dims):
    return jax.ShapeDtypeStruct(dims, F32)


def call(kernel, plan, outs, scratch, name, space=pltpu.VMEM):
    held = pl.BlockSpec(memory_space=pltpu.VMEM)
    return lambda *args: pl.pallas_call(
        functools.partial(kernel, plan), out_shape=outs, scratch_shapes=scratch, name=name,
        in_specs=[pl.BlockSpec(memory_space=space)] * len(args),
        out_specs=jax.tree.map(lambda _: held, outs),
        compiler_params=pltpu.CompilerParams(vmem_limit_bytes=VMEM_LIMIT),
    )(*args)


def vmem(*dims):
    return pltpu.VMEM(dims, F32)


def on_device(tracer, east, north, speed):
    bins, one, rows, lons = tracer.shape
    n, bands = lax.axis_size("lev"), lax.axis_size("lat")
    plan = Plan(bins, rows, lons, n)
    tiles, frame = plan.tiles, rows + 4 * SUB
    tracer, speed = tracer.reshape(bins, rows, lons), speed.reshape(bins, rows, lons)
    east, north = east.reshape(rows, lons), north.reshape(rows, lons)

    band = shape(tiles, SUB * plan.halo_groups, LANE)
    edge = 2 * rows + 2 * SUB * bins
    q1, ce, ns, up, down = call(
        start_kernel, plan,
        (shape(bins, tiles, rows, LANE), shape(3, tiles, rows, LANE), shape(tiles, rows, LANE), band, band),
        (
            vmem(bins * rows, lons), vmem(edge, lons), vmem(2, lons, LANE),
            vmem(tiles, bins * rows, LANE), vmem(tiles, edge, LANE),
            pltpu.SemaphoreType.DMA((3 * bins + 2,)),
        ),
        "start", pl.ANY,
    )(*(pltpu.with_memory_space_constraint(x, pltpu.HBM) for x in (tracer, east, north, speed)))
    south = lax.ppermute(up, "lat", [(i, i + 1) for i in range(bands - 1)])
    above = lax.ppermute(down, "lat", [(i + 1, i) for i in range(bands - 1)])

    def exchanged(parts):
        return [parts[0]] + [
            lax.ppermute(parts[k], "lev", [(i, i ^ k) for i in range(n)]) for k in range(1, n)
        ]

    part = shape(SUB * plan.message, LANE)
    every = vmem(n, SUB * plan.message, LANE)
    speeds = exchanged(
        call(
            speed_kernel, plan, (part,) * n,
            (vmem(lons, LANE), vmem(tiles, bins * rows, LANE), every), "speed",
        )(speed.reshape(bins * rows, lons))
    )

    buf = vmem(bins, tiles, frame + 2 * SUB, LANE)
    *parts, ceh, cn = call(
        advect_kernel, plan,
        (part,) * n + (shape(3, tiles, SUB, LANE), shape(3, tiles, frame, LANE)),
        (buf, buf, vmem(frame, LANE), vmem(3, tiles, 4 * SUB, LANE), every), "advect",
    )(q1, ce, ns, south, above)
    fields = exchanged(parts)

    deposited, *parts = call(
        settle_kernel, plan, (part,) + (part,) * n, (every, every, every), "settle"
    )(*fields, *speeds)
    parts = exchanged(parts)
    local = tiles * plan.width
    deposit = call(
        deposit_kernel, plan, shape(bins, rows, local),
        (vmem(bins * rows, LANE), vmem(-(-local // LANE) * LANE, LANE)), "deposit",
    )(deposited)

    out = call(
        close_kernel, plan, shape(bins, rows, lons),
        (
            every, vmem(bins, tiles, rows + SUB, LANE), vmem(bins, tiles, frame, LANE),
            vmem(tiles, bins * rows, LANE), vmem(lons, LANE),
        ),
        "close",
    )(ce, ceh, cn, *parts)
    return out.reshape(bins, one, rows, lons), deposit


def solution(mesh):
    in_specs = (
        P(None, "lev", "lat", None),
        P("lev", "lat", None),
        P("lev", "lat", None),
        P(None, "lev", "lat", None),
    )
    out_specs = (P(None, "lev", "lat", None), P(None, "lat", "lev"))
    return jax.shard_map(
        on_device, mesh=mesh, in_specs=in_specs, out_specs=out_specs, check_vma=False
    )
```

```python
import functools
import jax
import jax.numpy as jnp
from jax import lax
from jax.experimental import pallas as pl
from jax.experimental.pallas import tpu as pltpu
from jax.sharding import PartitionSpec as P

HSUB = 4
SETTLE_SUBSTEPS = 6
SUB = 8
LANE = 128
F32 = jnp.float32
VMEM_LIMIT = 16 << 20


def loop(count, body, unroll=1):
    def step(i, carry):
        body(i)
        return carry

    lax.fori_loop(0, count, step, 0, unroll=unroll)


def group(i):
    if isinstance(i, int):
        return pl.ds(SUB * i, SUB)
    return pl.ds(pl.multiple_of(SUB * i, SUB), SUB)


def roll(x, shift, axis):
    shift %= x.shape[axis]
    return pltpu.roll(x, shift, axis) if shift else x


def sublanes():
    return lax.broadcasted_iota(jnp.int32, (SUB, LANE), 0)


def lanes():
    return lax.broadcasted_iota(jnp.int32, (SUB, LANE), 1)


def coefficients(k):
    s = jnp.abs(k)
    r = 1.0 - s
    ks = k * s
    return k * (r * r), -(ks * r), ks * (3.0 - 2.0 * s)


def face(a, b, c, d):
    interp = (7.0 / 12.0) * (b + c) - (1.0 / 12.0) * (a + d)
    return jnp.minimum(jnp.maximum(interp, jnp.minimum(b, c)), jnp.maximum(b, c))


def flux(co, f, f_below, f_above, below, q):
    al, be, ga = co
    up = al >= 0
    return al * f + be * jnp.where(up, f_below, f_above) + ga * jnp.where(up, below, q)


def zonal(q, co):
    count = len(q)
    e = [roll(q[-2], 1, 1), roll(q[-1], 1, 1), *q, roll(q[0], -1, 1)]
    f = [face(*e[p : p + 4]) for p in range(count)]
    f = [roll(f[-1], 1, 1), *f, roll(f[0], -1, 1)]
    w = [flux(co[p], f[p + 1], f[p], f[p + 2], e[p + 1], q[p]) for p in range(count)]
    w.append(roll(w[0], -1, 1))
    return [q[p] - (w[p + 1] - w[p]) for p in range(count)]


def meridional(q, below2, below, above, co):
    f = face(below2, below, q, above)
    w = flux(co, f, roll(f, 1, 0), roll(f, -1, 0), below, q)
    return q - (roll(w, -1, 0) - w)


class Plan:
    def __init__(self, bins, rows, lons, count):
        self.bins, self.rows, self.lons, self.count = bins, rows, lons, count
        self.groups, self.tiles = rows // SUB, lons // LANE
        self.width = LANE // count
        self.vectors = -(-(self.groups + 2) // count)
        self.message = self.tiles * self.vectors
        self.halo_groups = 2 * bins + 3 + (bins + 1) // 2

    def at(self, b, p, v):
        return group((b * self.tiles + p) * self.vectors + v)


def interleave(plan, src, turned, put):
    rows = src.shape[0]
    for t in range(plan.tiles):
        turned[pl.ds(LANE * t, LANE), :rows] = src[:, LANE * t : LANE * (t + 1)].T
    for p in range(plan.tiles):
        put(p, turned[pl.ds(p, LANE, stride=plan.tiles), :].T[:rows])


def scatter(plan, xs):
    out = []
    for j in range(plan.count):
        y = roll(xs[0], -j * plan.width, 1)
        for s in range(1, len(xs)):
            y = jnp.where(lanes() < s * plan.width, y, roll(xs[s], (s - j) * plan.width, 1))
        out.append(y)
    return out


def gather(plan, ys, slot):
    x = roll(ys[0], -slot * plan.width, 1)
    for j in range(1, plan.count):
        x = jnp.where(lanes() < j * plan.width, x, roll(ys[j], (j - slot) * plan.width, 1))
    return x


def pack(plan, chunks, b, p, xs):
    for v in range(0, len(xs), plan.count):
        for j, y in enumerate(scatter(plan, xs[v : v + plan.count])):
            chunks[j, plan.at(b, p, v // plan.count), :] = y


def start_kernel(
    plan, tracer, east, north, speed, q1, ce, ns, first, second, x0, x1, turned, s0, s1, sem
):
    bins, rows, tiles, top = plan.bins, plan.rows, plan.tiles, plan.groups - 1
    moves = [(tracer.at[b], x0.at[pl.ds(b * rows, rows)]) for b in range(bins)]
    moves.append((east, x1.at[pl.ds(0, rows)]))
    moves.append((north, x1.at[pl.ds(rows, rows)]))
    edge = 2 * plan.groups
    for b in range(bins):
        for half, g in enumerate((0, top)):
            moves.append((speed.at[b, group(g)], x1.at[group(edge + 2 * b + half)]))
    copies = [pltpu.make_async_copy(*m, sem.at[i]) for i, m in enumerate(moves)]
    for c in copies:
        c.start()
    for c in copies[:bins]:
        c.wait()

    def put0(p, v):
        s0[p] = v

    def put1(p, v):
        s1[p] = v

    interleave(plan, x0, turned.at[0], put0)
    for c in copies[bins:]:
        c.wait()
    interleave(plan, x1, turned.at[1], put1)

    def body(g):
        k = [s1[p, group(g), :] for p in range(tiles)]
        co = [coefficients(c) for c in [roll(k[-1], 1, 1), *k[:-1]]]
        for p in range(tiles):
            for i in range(3):
                ce[i, p, group(g), :] = co[p][i]
        for b in range(bins):
            q = zonal([s0[p, group(b * plan.groups + g), :] for p in range(tiles)], co)
            for p in range(tiles):
                q1[b, p, group(g + 1), :] = q[p]

    loop(plan.groups, body, 2)
    sub = sublanes()
    base = 2 * bins

    def message(up, down, p):
        ns[p] = s1[p, pl.ds(rows, rows), :]
        east_at = lambda g: s1[p, group(g), :]
        north_at = lambda g: s1[p, group(plan.groups + g), :]
        speed_at = lambda b, half: s1[p, group(edge + 2 * b + half), :]
        for b in range(bins):
            for half in range(2):
                v = q1[b, p, group(top + half), :]
                if b == 0 and half == 0:
                    v = jnp.where(sub == 0, roll(north_at(top - 1), -3, 0), v)
                up[p, group(2 * b + half), :] = v
                down[p, group(2 * b + half), :] = q1[b, p, group(1 + half), :]
        up[p, group(base), :] = east_at(top)
        up[p, group(base + 1), :] = north_at(top)
        up[p, group(base + 2), :] = jnp.where(
            sub < 4, roll(east_at(top - 1), 4, 0), north_at(top - 1)
        )
        down[p, group(base), :] = east_at(0)
        down[p, group(base + 1), :] = north_at(0)
        down[p, group(base + 2), :] = jnp.where(sub < 4, east_at(1), roll(north_at(1), 4, 0))
        for h in range((bins + 1) // 2):
            a, b = 2 * h, min(2 * h + 1, bins - 1)
            up[p, group(base + 3 + h), :] = jnp.where(
                sub < 4, roll(speed_at(b, 1), 4, 0), speed_at(a, 1)
            )
            down[p, group(base + 3 + h), :] = jnp.where(
                sub < 4, speed_at(a, 0), roll(speed_at(b, 0), 4, 0)
            )

    even = lax.axis_index("lat") % 2 == 0

    @pl.when(even)
    def _():
        loop(tiles, functools.partial(message, first, second))

    @pl.when(jnp.logical_not(even))
    def _():
        loop(tiles, functools.partial(message, second, first))


def speed_kernel(plan, speed, *refs):
    outs, (turned, s, chunks) = refs[:-3], refs[-3:]
    me = lax.axis_index("lev")

    def put(p, v):
        s[p] = v

    interleave(plan, speed, turned, put)

    def body(p):
        for b in range(plan.bins):
            xs = [s[p, group(b * plan.groups + g), :] for g in range(plan.groups)]
            pack(plan, chunks, b, p, xs)

    loop(plan.tiles, body)
    for k in range(plan.count):
        outs[k][...] = chunks[me ^ k]


def inner_kernel(plan, q1, ce, ns, zs, q4, cn, frame):
    bins, groups, tiles, rows = plan.bins, plan.groups, plan.tiles, plan.rows

    def sweep(src, dst, pad, first):
        def body(p):
            if first:
                for i, c in enumerate(coefficients(roll(ns[p], 1, 0))):
                    cn[i, p] = c
            co = [cn[i, p] for i in range(3)]
            for b in range(bins):
                q, below2, below, beyond = (
                    src[b, p, pl.ds(SUB + d, rows), :] for d in (0, -2, -1, 1)
                )
                dst[b, p, pl.ds(pad, rows), :] = meridional(q, below2, below, beyond, co)

        loop(tiles, body)

    sweep(q1, frame, SUB, True)
    for step in range(HSUB - 1):

        def body(g):
            co = [[ce[i, p, group(g), :] for i in range(3)] for p in range(tiles)]
            for b in range(bins):
                q = zonal([frame[b, p, group(g + 1), :] for p in range(tiles)], co)
                for p in range(tiles):
                    zs[step, b, p, group(g + 1), :] = q[p]

        loop(groups, body, 2)
        last = step == HSUB - 2
        sweep(zs.at[step], q4 if last else frame, 0 if last else SUB, False)


def halo_kernel(plan, first, second, ce, ns, rim, fh, ceh, ceside, cnside, halo):
    bins, groups, tiles = plan.bins, plan.groups, plan.tiles
    base = 2 * bins
    sub = sublanes()
    last = lax.axis_index("lat") == lax.axis_size("lat") - 1
    closed = jnp.logical_and(last, sub == SUB - 1)

    def fill(south, above):
        def body(p):
            for b in range(bins):
                for half in range(2):
                    rim[b, p, group(half), :] = south[p, group(2 * b + half), :]
                    rim[b, p, group(2 + half), :] = above[p, group(2 * b + half), :]
                at = group(base + 3 + b // 2)
                parts = above[p, at, :], south[p, at, :]
                if b % 2:
                    parts = [roll(v, 4, 0) for v in parts]
                fh[b, p] = jnp.where(sub < 4, *parts)
            low = [
                jnp.where(sub == 3, roll(south[p, group(0), :], 3, 0), south[p, group(base + 2), :]),
                south[p, group(base + 1), :],
                ns[p, group(0), :],
                ns[p, group(1), :],
            ]
            high = [
                ns[p, group(groups - 2), :],
                jnp.where(closed, 0.0, ns[p, group(groups - 1), :]),
                above[p, group(base + 1), :],
                roll(above[p, group(base + 2), :], 4, 0),
            ]
            for side, raw in enumerate((low, high)):
                k = roll(jnp.concatenate(raw, 0), 1, 0)
                for i, c in enumerate(coefficients(k)):
                    cnside[i, p, pl.ds(4 * SUB * side, 4 * SUB), :] = c

        loop(tiles, body)
        courants = (
            [roll(south[p, group(base + 2), :], 4, 0) for p in range(tiles)],
            [south[p, group(base), :] for p in range(tiles)],
            [above[p, group(base), :] for p in range(tiles)],
            [above[p, group(base + 2), :] for p in range(tiles)],
        )
        for g, k in enumerate(courants):
            for p, c in enumerate([roll(k[-1], 1, 1), *k[:-1]]):
                for i, v in enumerate(coefficients(c)):
                    ceside[i, p, group(g), :] = v

    even = lax.axis_index("lat") % 2 == 0

    @pl.when(even)
    def _():
        fill(second, first)

    @pl.when(jnp.logical_not(even))
    def _():
        fill(first, second)

    for p in range(tiles):
        for i in range(3):
            ceh[i, p] = jnp.where(sub < 4, ceside[i, p, group(2), :], ceside[i, p, group(1), :])


def edge_kernel(plan, b, q1, zs, q4, ce, rim, fh, ceside, cnside, *refs):
    outs, (fa, fb, chunks) = refs[: plan.count], refs[plan.count :]
    groups, tiles = plan.groups, plan.tiles
    sub = sublanes()
    me = lax.axis_index("lev")
    core = ((None, None, 0, 1), (groups - 2, groups - 1, None, None))
    rims = ((0, 1, None, None), (None, None, 2, 3))

    def fill(p):
        for side in range(2):
            for g in range(4):
                c = core[side][g]
                v = rim[b, p, group(rims[side][g]), :] if c is None else q1[b, p, group(c + 1), :]
                fa[side, p, group(g + 1), :] = v

    loop(tiles, fill)

    def lowest(side, step):
        return int(step >= 3) if side == 0 else int(step < 3)

    def meridional_sweep(step):
        def body(p):
            for side in range(2):
                low = lowest(side, step)
                at = SUB * (1 + low)
                co = [cnside[i, p, pl.ds(SUB * (4 * side + low), 3 * SUB), :] for i in range(3)]
                q, below2, below, beyond = (
                    fa[side, p, pl.ds(at + d, 3 * SUB), :] for d in (0, -2, -1, 1)
                )
                fb[side, p, pl.ds(at, 3 * SUB), :] = meridional(q, below2, below, beyond, co)

        loop(tiles, body)

    def zonal_sweep(step):
        reach = 3 * (step - 1)
        for side in range(2):
            low = lowest(side, step - 1)
            for g in range(4):
                c = core[side][g]
                inner = [] if c is None else [
                    zs[step - 2, b, p, group(c + 1), :] for p in range(tiles)
                ]
                if low <= g < low + 3:
                    table, index = (ceside, rims[side][g]) if c is None else (ce, c)
                    co = [[table[i, p, group(index), :] for i in range(3)] for p in range(tiles)]
                    q = zonal([fb[side, p, group(g + 1), :] for p in range(tiles)], co)
                    if c is not None:
                        ours = sub + SUB * c < reach
                        if side:
                            ours = sub + SUB * c >= plan.rows - reach
                        q = [jnp.where(ours, x, y) for x, y in zip(q, inner)]
                elif c is None:
                    continue
                else:
                    q = inner
                for p in range(tiles):
                    fa[side, p, group(g + 1), :] = q[p]

    meridional_sweep(1)
    for step in range(2, HSUB + 1):
        zonal_sweep(step)
        meridional_sweep(step)

    def columns(p):
        low = [fb[0, p, group(g + 1), :] for g in range(1, 4)]
        high = [fb[1, p, group(g + 1), :] for g in range(3)]
        xs = [q4[b, p, group(g), :] for g in range(groups)]
        xs[0] = low[1]
        xs[1] = jnp.where(sub < 4, low[2], xs[1])
        xs[groups - 2] = jnp.where(sub < 4, xs[groups - 2], high[0])
        xs[groups - 1] = high[1]
        xs.append(jnp.where(sub < 4, high[2], low[0]))
        xs.append(fh[b, p])
        pack(plan, chunks, 0, p, xs)

    loop(tiles, columns)
    for k in range(plan.count):
        outs[k][...] = chunks[me ^ k]


def settle_kernel(plan, b, *refs):
    n, groups = plan.count, plan.groups
    fields, speeds, deposited = refs[:n], refs[n : 2 * n], refs[2 * n]
    outs = refs[2 * n + 1 : 3 * n + 1]
    fld, fal, res = refs[3 * n + 1 :]
    me = lax.axis_index("lev")
    for k in range(n):
        fld[me ^ k] = fields[k][...]
        fal[me ^ k] = speeds[k][pl.ds(b * SUB * plan.message, SUB * plan.message), :]
    halo, halo_slot = divmod(groups, n)
    speed, speed_slot = divmod(groups + 1, n)
    low, high = halo_slot * plan.width, (halo_slot + 1) * plan.width
    here = jnp.logical_and(lanes() >= low, lanes() < high)

    def body(i):
        for vector in range(plan.vectors):
            rows = group(i * plan.vectors + vector)
            q = [fld[l, rows, :] for l in range(n)]
            v = [fal[l, rows, :] for l in range(n)]
            if vector == halo:
                own = group(i * plan.vectors + speed)
                turn = (halo_slot - speed_slot) * plan.width
                v = [jnp.where(here, roll(fld[l, own, :], turn, 1), v[l]) for l in range(n)]
            h = [0.5 * x for x in v]
            total = None
            for _ in range(SETTLE_SUBSTEPS):
                inflow = None
                for l in range(n):
                    down = (v[l] + h[l] * jnp.tanh(q[l])) * q[l]
                    q[l] = (q[l] if inflow is None else q[l] + inflow) - down
                    inflow = down
                total = inflow if total is None else total + inflow
            for l in range(n):
                res[l, rows, :] = q[l]
            deposited[rows, :] = total

    loop(plan.tiles, body, 3)
    for k in range(n):
        outs[k][...] = res[me ^ k]


def deposit_kernel(plan, *refs):
    deposited, (deposit, side, turned) = refs[: plan.bins], refs[plan.bins :]
    n, groups, tiles, width = plan.count, plan.groups, plan.tiles, plan.width
    rows = plan.bins * plan.rows
    for first in range(0, tiles, n):
        held = range(first, min(first + n, tiles))
        for b in range(plan.bins):
            for g in range(groups):
                y = None
                for s, p in enumerate(held):
                    x = deposited[b][plan.at(0, p, g // n), :]
                    x = roll(x, (s - g % n) * width, 1)
                    y = x if y is None else jnp.where(lanes() < s * width, y, x)
                side[group(b * groups + g), :] = y
        x = side[...].T
        for s, p in enumerate(held):
            turned[pl.ds(p, width, stride=tiles), :rows] = x[s * width : (s + 1) * width]
    lons = tiles * width
    for t in range(-(-lons // LANE)):
        x = turned[pl.ds(LANE * t, LANE), :].T[:rows]
        end = min(LANE * (t + 1), lons)
        for b in range(plan.bins):
            deposit[b, :, LANE * t : end] = x[b * plan.rows : (b + 1) * plan.rows, : end - LANE * t]


def close_kernel(plan, b, ce, ceh, cn, cnside, *refs):
    n, groups, tiles = plan.count, plan.groups, plan.tiles
    ins = refs[:n]
    out, parts, spread, frame, done, turned, ready, sem = refs[n + (b > 0) :]
    me = lax.axis_index("lev")
    for k in range(n):
        parts[me ^ k] = ins[k][...]

    def place(p):
        for g in range(groups + 1):
            ys = [parts[j, plan.at(0, p, g // n), :] for j in range(n)]
            spread[p, group(g), :] = gather(plan, ys, g % n)

    loop(tiles, place)

    def row_group(g, table, index, targets):
        co = [[table[i, p, group(index), :] for i in range(3)] for p in range(tiles)]
        q = zonal([spread[p, group(g), :] for p in range(tiles)], co)
        for p in range(tiles):
            for a in targets:
                frame[p, group(a), :] = q[p]

    loop(groups, lambda g: row_group(g, ce, g, (g + 2,)), 3)
    row_group(groups, ceh, 0, (1, groups + 2))
    rows = plan.rows + 2 * SUB

    def body(p):
        co = [
            jnp.concatenate(
                [
                    cnside[i, p, pl.ds(SUB, 2 * SUB), :],
                    cn[i, p, pl.ds(SUB, plan.rows - SUB), :],
                    cnside[i, p, pl.ds(6 * SUB, SUB), :],
                ],
                0,
            )
            for i in range(3)
        ]
        q, below2, below, beyond = (frame[p, pl.ds(SUB + d, rows), :] for d in (0, -2, -1, 1))
        done[p] = meridional(q, below2, below, beyond, co)[SUB : SUB + plan.rows]

    loop(tiles, body, 3)
    for p in range(tiles):
        turned[pl.ds(p, LANE, stride=tiles), : plan.rows] = done[p].T
    copies = []
    for t in range(tiles):
        cut = pl.ds(LANE * t, LANE)
        ready[:, cut] = turned[cut, :].T[: plan.rows]
        copies.append(pltpu.make_async_copy(ready.at[:, cut], out.at[b, :, cut], sem.at[t]))
        copies[-1].start()
    for c in copies:
        c.wait()


def shape(*dims):
    return jax.ShapeDtypeStruct(dims, F32)


def call(kernel, plan, outs, scratch, hbm_in=(), hbm_out=False, alias={}):
    held = pl.BlockSpec(memory_space=pltpu.VMEM)
    far = pl.BlockSpec(memory_space=pltpu.HBM)
    return lambda *args: pl.pallas_call(
        functools.partial(kernel, plan), out_shape=outs, scratch_shapes=scratch,
        in_specs=[far if i in hbm_in else held for i in range(len(args))],
        out_specs=jax.tree.map(lambda _: far if hbm_out else held, outs),
        compiler_params=pltpu.CompilerParams(vmem_limit_bytes=VMEM_LIMIT),
        input_output_aliases=alias,
    )(*args)


def vmem(*dims):
    return pltpu.VMEM(dims, F32)


def window(tracer, east, north, speed):
    bins, one, rows, lons = tracer.shape
    n, bands = lax.axis_size("lev"), lax.axis_size("lat")
    plan = Plan(bins, rows, lons, n)
    tiles, frame = plan.tiles, rows + 4 * SUB
    tracer, speed = tracer.reshape(bins, rows, lons), speed.reshape(bins, rows, lons)
    east, north = east.reshape(rows, lons), north.reshape(rows, lons)

    band = shape(tiles, SUB * plan.halo_groups, LANE)
    padded = (bins, tiles, rows + 2 * SUB, LANE)
    edge = 2 * rows + 2 * SUB * bins
    q1, ce, ns, first, second = call(
        start_kernel, plan,
        (shape(*padded), shape(3, tiles, rows, LANE), shape(tiles, rows, LANE), band, band),
        (
            vmem(bins * rows, lons), vmem(edge, lons), vmem(2, lons, LANE),
            vmem(tiles, bins * rows, LANE), vmem(tiles, edge, LANE),
            pltpu.SemaphoreType.DMA((3 * bins + 2,)),
        ),
        range(4),
    )(*(pltpu.with_memory_space_constraint(x, pltpu.HBM) for x in (tracer, east, north, speed)))
    pairs = [(i, i ^ 1) for i in range(bands) if i ^ 1 < bands]
    first = lax.ppermute(first, "lat", pairs)
    pairs = [(i, ((i + 1) ^ 1) - 1) for i in range(1, bands) if ((i + 1) ^ 1) - 1 < bands]
    second = lax.ppermute(second, "lat", pairs)

    def exchanged(parts):
        return [parts[0]] + [
            lax.ppermute(parts[k], "lev", [(i, i ^ k) for i in range(n)]) for k in range(1, n)
        ]

    part = shape(bins * SUB * plan.message, LANE)
    speeds = exchanged(
        call(
            speed_kernel, plan, (part,) * n,
            (
                vmem(lons, LANE), vmem(tiles, bins * rows, LANE),
                vmem(n, bins * SUB * plan.message, LANE),
            ),
        )(speed.reshape(bins * rows, lons))
    )

    zs, q4, cn = call(
        inner_kernel, plan,
        (shape(HSUB - 1, *padded), shape(bins, tiles, rows, LANE), shape(3, tiles, rows, LANE)),
        (vmem(*padded),),
    )(q1, ce, ns)
    rim, fh, ceh, ceside, cnside = call(
        halo_kernel, plan,
        (
            shape(bins, tiles, 4 * SUB, LANE), shape(bins, tiles, SUB, LANE),
            shape(3, tiles, SUB, LANE), shape(3, tiles, 4 * SUB, LANE),
            shape(3, tiles, 8 * SUB, LANE),
        ),
        (vmem(SUB, LANE),),
    )(first, second, ce, ns)

    part = shape(SUB * plan.message, LANE)
    every = vmem(n, SUB * plan.message, LANE)
    side = vmem(2, tiles, 6 * SUB, LANE)
    fields = [
        exchanged(
            call(
                lambda plan, *refs, b=b: edge_kernel(plan, b, *refs), plan, (part,) * n,
                (side, side, every),
            )(q1, zs, q4, ce, rim, fh, ceside, cnside)
        )
        for b in range(bins)
    ]
    deposited, settled = [], []
    for b in range(bins):
        total, *parts = call(
            lambda plan, *refs, b=b: settle_kernel(plan, b, *refs), plan, (part,) + (part,) * n,
            (every, every, every),
        )(*fields[b], *speeds)
        deposited.append(total)
        settled.append(exchanged(parts))
    local = tiles * plan.width
    deposit = call(
        deposit_kernel, plan, shape(bins, rows, local),
        (vmem(bins * rows, LANE), vmem(-(-local // LANE) * LANE, LANE)),
    )(*deposited)

    out = []
    for b in range(bins):
        out = [
            call(
                lambda plan, *refs, b=b: close_kernel(plan, b, *refs), plan,
                shape(bins, rows, lons),
                (
                    every, vmem(tiles, rows + SUB, LANE), vmem(tiles, frame, LANE),
                    vmem(tiles, rows, LANE), vmem(lons, LANE), vmem(rows, lons),
                    pltpu.SemaphoreType.DMA((tiles,)),
                ),
                (4 + n,), True, {4 + n: 0} if out else {},
            )(ce, ceh, cn, cnside, *settled[b], *out)
        ]
    return out[0].reshape(bins, one, rows, lons), deposit


def solution(mesh):
    in_specs = (
        P(None, "lev", "lat", None),
        P("lev", "lat", None),
        P("lev", "lat", None),
        P(None, "lev", "lat", None),
    )
    out_specs = (P(None, "lev", "lat", None), P(None, "lat", "lev"))
    return jax.shard_map(window, mesh=mesh, in_specs=in_specs, out_specs=out_specs, check_vma=False)
```

```python
import functools
import jax
import jax.numpy as jnp
from jax import lax
from jax.experimental import pallas as pl
from jax.experimental.pallas import tpu as pltpu
from jax.sharding import PartitionSpec as P

HSUB = 4
SETTLE_SUBSTEPS = 6
SUB = 8
LANE = 128
F32 = jnp.float32
VMEM_LIMIT = 16 << 20


def loop(count, body, unroll=1):
    def step(i, carry):
        body(i)
        return carry

    lax.fori_loop(0, count, step, 0, unroll=unroll)


def group(i):
    if isinstance(i, int):
        return pl.ds(SUB * i, SUB)
    return pl.ds(pl.multiple_of(SUB * i, SUB), SUB)


def roll(x, shift, axis):
    shift %= x.shape[axis]
    return pltpu.roll(x, shift, axis) if shift else x


def sublanes():
    return lax.broadcasted_iota(jnp.int32, (SUB, LANE), 0)


def lanes():
    return lax.broadcasted_iota(jnp.int32, (SUB, LANE), 1)


def coefficients(k):
    s = jnp.abs(k)
    r = 1.0 - s
    ks = k * s
    return k * (r * r), -(ks * r), ks * (3.0 - 2.0 * s)


def face(a, b, c, d):
    interp = (7.0 / 12.0) * (b + c) - (1.0 / 12.0) * (a + d)
    return jnp.minimum(jnp.maximum(interp, jnp.minimum(b, c)), jnp.maximum(b, c))


def flux(co, f, f_below, f_above, below, q):
    al, be, ga = co
    up = al >= 0
    return al * f + be * jnp.where(up, f_below, f_above) + ga * jnp.where(up, below, q)


def west_courants(k):
    return [roll(k[-1], 1, 1), *k]


def zonal(q, co):
    count = len(q)
    e = [roll(v, 1, 1) for v in q[-3:]] + list(q) + [roll(v, -1, 1) for v in q[:3]]
    f = [face(*e[p : p + 4]) for p in range(count + 3)]
    w = [flux(co[p], f[p + 1], f[p], f[p + 2], e[p + 2], e[p + 3]) for p in range(count + 1)]
    return [q[p] - (w[p + 1] - w[p]) for p in range(count)]


def meridional(q, below2, below, above, co):
    f = face(below2, below, q, above)
    w = flux(co, f, roll(f, 1, 0), roll(f, -1, 0), below, q)
    return q - (roll(w, -1, 0) - w)


class Plan:
    def __init__(self, bins, rows, lons, count):
        self.bins, self.rows, self.lons, self.count = bins, rows, lons, count
        self.groups, self.tiles = rows // SUB, lons // LANE
        self.width = LANE // count
        self.outer = (0, 1, self.groups - 2, self.groups - 1)
        self.interior = tuple(range(2, self.groups - 2))
        self.n_outer = -(-self.tiles * len(self.outer) // count)
        self.n_halo = -(-self.tiles * 2 // count)
        self.n_back = -(-self.n_halo // 2)
        self.n_inner = -(-self.tiles * bins * len(self.interior) // count)
        self.n_speed = bins * self.n_outer + self.n_inner
        self.halo_rows = 2 * SUB * (bins + 2)

    def back(self, b):
        return self.n_outer + self.n_back + (0 if b else self.n_inner)

    def outer_blocks(self, b):
        return [(b, p, g) for p in range(self.tiles) for g in self.outer]

    def halo_blocks(self, b):
        return [(b, p, self.groups + i) for p in range(self.tiles) for i in range(2)]

    def inner_blocks(self):
        return [
            (b, p, g) for p in range(self.tiles) for b in range(self.bins) for g in self.interior
        ]

    def find(self, b, p, g):
        if g in self.interior:
            first, at = self.n_outer + self.n_back, self.inner_blocks().index((b, p, g))
            b = 0
        elif g >= self.groups:
            vector, slot = divmod(self.halo_blocks(b).index((b, p, g)), self.count)
            return b, self.n_outer + vector // 2, slot + vector % 2
        else:
            first, at = 0, self.outer_blocks(b).index((b, p, g))
        return b, first + at // self.count, at % self.count


def interleave(plan, src, turned, put):
    rows = src.shape[0]
    for t in range(plan.tiles):
        turned[pl.ds(LANE * t, LANE), :rows] = src[:, LANE * t : LANE * (t + 1)].T
    for p in range(plan.tiles):
        put(p, turned[pl.ds(p, LANE, stride=plan.tiles), :].T[:rows])


def scatter(plan, xs):
    out = []
    for j in range(plan.count):
        y = roll(xs[0], -j * plan.width, 1)
        for s in range(1, len(xs)):
            y = jnp.where(lanes() < s * plan.width, y, roll(xs[s], (s - j) * plan.width, 1))
        out.append(y)
    return out


def gather(plan, ys, slot):
    x = roll(ys[0], -slot * plan.width, 1)
    for j in range(1, plan.count):
        x = jnp.where(lanes() < j * plan.width, x, roll(ys[j], (j - slot) * plan.width, 1))
    return x


def pack(plan, chunks, first, blocks, load):
    for v in range(0, len(blocks), plan.count):
        xs = [load(*block) for block in blocks[v : v + plan.count]]
        for j, y in enumerate(scatter(plan, xs)):
            chunks[j, group(first + v // plan.count), :] = y


def rows_kernel(plan, tracer, east, north, speed, first, second, x, turned, ends, sem):
    bins, rows, top = plan.bins, plan.rows, plan.groups - 1
    sub = lax.broadcasted_iota(jnp.int32, (SUB, plan.lons), 0)
    base, pair = 2 * bins, 2 * SUB

    def run(up, down):
        moves = [
            (speed.at[b, group(g)], ends.at[b, i]) for b in range(bins) for i, g in ((0, 0), (1, top))
        ]
        for ref, low in ((up, rows - pair), (down, 0)):
            cut = pl.ds(low, pair)
            moves += [(tracer.at[b, cut], ref.at[pl.ds(pair * b, pair)]) for b in range(bins)]
            moves.append((east.at[cut], ref.at[pl.ds(pair * bins, pair)]))
            moves.append((north.at[cut], ref.at[pl.ds(pair * (bins + 1), pair)]))
        copies = [pltpu.make_async_copy(*m, sem.at[i]) for i, m in enumerate(moves)]
        for c in copies:
            c.start()
        for c in copies:
            c.wait()

        def merge(ref, g, where, value):
            ref[group(g), :] = jnp.where(where, value, ref[group(g), :])

        merge(up, base + 2, sub < 3, roll(ends[0, 1], -5, 0))
        merge(down, base + 3, jnp.logical_and(sub >= 4, sub < 7), roll(ends[0, 0], 4, 0))
        if bins > 1:
            for k, g in enumerate((0, 2, base)):
                merge(up, g, sub == 0, roll(ends[1, 1], -5 - k, 0))
                merge(down, g + 1, sub == 7, roll(ends[1, 0], 7 - k, 0))

    count = plan.halo_rows
    refs = x.at[pl.ds(0, count)], x.at[pl.ds(count, count)]
    on_even(lambda refs: run(*refs), refs, refs[::-1])

    def put(p, v):
        first[p] = v[:count]
        second[p] = v[count:]

    interleave(plan, x, turned, put)


def start_kernel(plan, tracer, east, north, speed, q1, ce, ns, held, x0, x1, turned, s0, s1, sem):
    bins, rows, tiles = plan.bins, plan.rows, plan.tiles
    moves = [(tracer.at[b], x0.at[pl.ds(b * rows, rows)]) for b in range(bins)]
    moves.append((east, x1.at[pl.ds(0, rows)]))
    moves.append((north, x1.at[pl.ds(rows, rows)]))
    moves.append((speed, held))
    copies = [pltpu.make_async_copy(*m, sem.at[i]) for i, m in enumerate(moves)]
    for c in copies:
        c.start()
    for c in copies[:bins]:
        c.wait()

    def put0(p, v):
        s0[p] = v

    def put1(p, v):
        s1[p] = v[:rows]
        ns[p] = v[rows:]

    interleave(plan, x0, turned.at[0], put0)
    for c in copies[bins:-1]:
        c.wait()
    interleave(plan, x1, turned.at[1], put1)

    def body(g):
        co = [coefficients(c) for c in west_courants([s1[p, group(g), :] for p in range(tiles)])]
        for p in range(tiles + 1):
            for i in range(3):
                ce[i, p, group(g), :] = co[p][i]
        for b in range(bins):
            q = zonal([s0[p, group(b * plan.groups + g), :] for p in range(tiles)], co)
            for p in range(tiles):
                q1[b, p, group(g + 1), :] = q[p]

    loop(plan.groups, body, plan.groups)
    copies[-1].wait()


def speed_kernel(plan, speed, q4, *refs):
    outs, (turned, s, chunks) = refs[:-3], refs[-3:]
    me = lax.axis_index("lev")

    def put(p, v):
        s[p] = v

    interleave(plan, speed, turned, put)

    def load(b, p, g):
        return s[p, group(b * plan.groups + g), :]

    for b in range(plan.bins):
        pack(plan, chunks, b * plan.n_outer, plan.outer_blocks(b), load)
    pack(plan, chunks, plan.bins * plan.n_outer, plan.inner_blocks(), load)

    def field(b, p, g):
        return q4[b, p, group(g), :]

    pack(plan, chunks, plan.n_speed, plan.inner_blocks(), field)
    for k in range(plan.count):
        outs[k][...] = chunks[me ^ k]


def inner_kernel(plan, q1, ce, ns, zs, q4, cn, frame):
    bins, groups, tiles, rows = plan.bins, plan.groups, plan.tiles, plan.rows

    def sweep(src, dst, pad, low):
        cut = rows - 2 * SUB * low

        def body(p):
            if src is q1:
                for i, c in enumerate(coefficients(roll(ns[p], 1, 0))):
                    cn[i, p] = c
            co = [cn[i, p, pl.ds(SUB * low, cut), :] for i in range(3)]
            for b in range(bins):
                q, below2, below, beyond = (
                    src[b, p, pl.ds(SUB * (1 + low) + d, cut), :] for d in (0, -2, -1, 1)
                )
                q = meridional(q, below2, below, beyond, co)
                dst[b, p, pl.ds(pad + SUB * low, cut), :] = q

        loop(tiles, body, tiles)

    sweep(q1, frame, SUB, 0)
    for step in range(HSUB - 1):
        low = 3 * (step + 1) // SUB

        def body(i):
            g = i + low
            co = [[ce[i, p, group(g), :] for i in range(3)] for p in range(tiles + 1)]
            for b in range(bins):
                q = zonal([frame[b, p, group(g + 1), :] for p in range(tiles)], co)
                for p in range(tiles):
                    zs[step, b, p, group(g + 1), :] = q[p]

        loop(groups - 2 * low, body, groups - 2 * low)
        last = step == HSUB - 2
        low = (3 * (step + 2) - 2) // SUB
        sweep(zs.at[step], q4 if last else frame, 0 if last else SUB, low)


def on_even(run, for_even, for_odd):
    even = lax.axis_index("lat") % 2 == 0

    @pl.when(even)
    def _():
        run(for_even)

    @pl.when(jnp.logical_not(even))
    def _():
        run(for_odd)

    return even


class Side:
    def __init__(self, plan, side):
        self.plan, self.side = plan, side
        top = plan.groups - 1
        self.core = (None, None, 0, 1) if side == 0 else (top - 1, top, None, None)
        self.rim = (0, 1, None, None) if side == 0 else (None, None, 0, 1)

    def lowest(self, step):
        return int(step >= 3) if self.side == 0 else int(step < 3)

    def prepare(self, sv, ns, ces, cns, fhs):
        plan, sub, side = self.plan, sublanes(), self.side
        bins, top, tiles = plan.bins, plan.groups - 1, plan.tiles
        base = 2 * bins
        last = lax.axis_index("lat") == lax.axis_size("lat") - 1
        closed = jnp.logical_and(last, sub == SUB - 1)

        for g in range(2):
            for p, c in enumerate(west_courants([sv[p, group(base + g), :] for p in range(tiles)])):
                for i, v in enumerate(coefficients(c)):
                    ces[i, p, group(g), :] = v

        def body(p):
            at = lambda g: sv[p, group(g), :]
            near = [at(base + 2), at(base + 3)]
            if side == 0:
                raw = near + [ns[p, group(0), :], ns[p, group(1), :]]
            else:
                end = jnp.where(closed, 0.0, ns[p, group(top), :])
                raw = [ns[p, group(top - 1), :], end] + near
            for i, c in enumerate(coefficients(roll(jnp.concatenate(raw, 0), 1, 0))):
                cns[i, p] = c
            fhs[0, p] = roll(near[side], 5 - side, 0)
            if bins > 1:
                parts = [
                    roll(at(g + side), k + 1 if side else k + 5, 0)
                    for k, g in enumerate((0, 2, base))
                ]
                lone = 0 if side else 5
                fhs[1, p] = jnp.where(
                    sub == lone, parts[0], jnp.where(sub == lone + 1, parts[1], parts[2])
                )

        loop(tiles, body, 3)

    def fill(self, sv, ces, b, q1, fa):
        tiles = self.plan.tiles

        def body(p):
            for g in range(4):
                c = self.core[g]
                if c is not None:
                    fa[p, group(g + 1), :] = q1[b, p, group(c + 1), :]

        loop(tiles, body, 3)
        for g in range(4):
            r = self.rim[g]
            if r is not None:
                co = [[ces[i, p, group(r), :] for i in range(3)] for p in range(tiles + 1)]
                q = zonal([sv[p, group(2 * b + r), :] for p in range(tiles)], co)
                for p in range(tiles):
                    fa[p, group(g + 1), :] = q[p]

    def meridional_sweep(self, step, bins, cns, fa, fb):
        low = self.lowest(step)
        at = SUB * (1 + low)

        def body(p):
            co = [cns[i, p, pl.ds(SUB * low, 3 * SUB), :] for i in range(3)]
            for b in range(bins):
                q, below2, below, beyond = (
                    fa[b, p, pl.ds(at + d, 3 * SUB), :] for d in (0, -2, -1, 1)
                )
                fb[b, p, pl.ds(at, 3 * SUB), :] = meridional(q, below2, below, beyond, co)

        tiles = self.plan.tiles
        loop(tiles, body, tiles)

    def zonal_sweep(self, step, bins, first, zs, ce, ces, fb, fa):
        plan, sub = self.plan, sublanes()
        tiles = plan.tiles
        reach, low = 3 * (step - 1), self.lowest(step - 1)
        for g in range(4):
            c = self.core[g]
            here = low <= g < low + 3
            if c is None and not here:
                continue
            if here:
                table, index = (ces, self.rim[g]) if c is None else (ce, c)
                co = [[table[i, p, group(index), :] for i in range(3)] for p in range(tiles + 1)]
            for b in range(bins):
                if c is not None:
                    q = inner = [zs[step - 2, first + b, p, group(c + 1), :] for p in range(tiles)]
                if here:
                    q = zonal([fb[b, p, group(g + 1), :] for p in range(tiles)], co)
                    if c is not None:
                        row = sub + SUB * c
                        ours = row >= plan.rows - reach if self.side else row < reach
                        q = [jnp.where(ours, x, y) for x, y in zip(q, inner)]
                for p in range(tiles):
                    fa[b, p, group(g + 1), :] = q[p]

    def advance(self, bins, first, zs, ce, ces, cns, fa, fb, result):
        self.meridional_sweep(1, bins, cns, fa, fb)
        for step in range(2, HSUB + 1):
            self.zonal_sweep(step, bins, first, zs, ce, ces, fb, fa)
            self.meridional_sweep(step, bins, cns, fa, fb)
        rows = pl.ds(SUB * (1 + self.lowest(HSUB)), 3 * SUB)

        def body(p):
            for b in range(bins):
                result[b, p] = fb[b, p, rows, :]

        loop(self.plan.tiles, body, 3)


def near_kernel(plan, message, q1, zs, ce, ns, result, ces, cns, fhs, fa, fb):
    def run(side):
        side.prepare(message, ns, ces, cns, fhs)
        for b in range(plan.bins):
            side.fill(message, ces, b, q1, fa.at[b])
        side.advance(plan.bins, 0, zs, ce, ces, cns, fa, fb, result)

    on_even(run, Side(plan, 0), Side(plan, 1))


def far_kernel(plan, b, message, q1, zs, q4, ce, ns, near, fhs, *refs):
    if b:
        far_fhs, ces, cns = refs[:3]
        outs, (fa, fb, result, chunks) = refs[3 : 3 + plan.count], refs[3 + plan.count :]
    else:
        outs = refs[: plan.count]
        far_fhs, ces, cns, fa, fb, result, chunks = refs[plan.count :]
    groups = plan.groups
    sub = sublanes()
    me = lax.axis_index("lev")

    def run(side):
        if b == 0:
            side.prepare(message, ns, ces, cns, far_fhs)
        side.fill(message, ces, b, q1, fa.at[0])
        side.advance(1, b, zs, ce, ces, cns, fa, fb, result)

    even = jnp.logical_not(on_even(run, Side(plan, 1), Side(plan, 0)))

    def load(c, p, g):
        ours, theirs = lambda i: near[b, p, group(i), :], lambda i: result[0, p, group(i), :]
        low = lambda i: jnp.where(even, theirs(i), ours(i))
        high = lambda i: jnp.where(even, ours(i), theirs(i))
        if g == 0:
            return low(1)
        if g == 1:
            return jnp.where(sub < 4, low(2), q4[b, p, group(1), :])
        if g == groups - 2:
            return jnp.where(sub < 4, q4[b, p, group(g), :], high(0))
        if g == groups - 1:
            return high(1)
        if g == groups:
            return jnp.where(sub < 4, high(2), low(0))
        x, y = fhs[b, p], far_fhs[b, p]
        return jnp.where(sub < 4, jnp.where(even, x, y), jnp.where(even, y, x))

    pack(plan, chunks, 0, plan.outer_blocks(b), load)
    pack(plan, chunks, plan.n_outer, plan.halo_blocks(b), load)
    for k in range(plan.count):
        outs[k][...] = chunks[me ^ k]


def settle_kernel(plan, b, *refs):
    n = plan.count
    fields, speeds, deposited = refs[:n], refs[n : 2 * n], refs[2 * n]
    outs = refs[2 * n + 1 : 3 * n + 1]
    fld, fal, res = refs[3 * n + 1 :]
    me = lax.axis_index("lev")
    for k in range(n):
        fld[me ^ k] = fields[k][...]
        fal[me ^ k] = speeds[k][...]

    def settle(first, count, speed_first, field=fld, field_first=None):
        def body(i):
            rows = group(first + i)
            at = rows if field_first is None else group(field_first + i)
            q = [field[l, at, :] for l in range(n)]
            if speed_first is None:
                v = [roll(x, -plan.width, 1) for x in q]
            else:
                v = [fal[l, group(speed_first + i), :] for l in range(n)]
            h = [0.5 * x for x in v]
            total = None
            for _ in range(SETTLE_SUBSTEPS):
                inflow = None
                for l in range(n):
                    down = (v[l] + h[l] * jnp.tanh(q[l])) * q[l]
                    q[l] = (q[l] if inflow is None else q[l] + inflow) - down
                    inflow = down
                total = inflow if total is None else total + inflow
            for l in range(n):
                res[l, rows, :] = q[l]
            if speed_first is not None:
                deposited[rows, :] = total

        loop(count, body, next(u for u in (5, 4, 3, 2, 1) if count % u == 0))

    settle(0, plan.n_outer, b * plan.n_outer)
    settle(plan.n_outer, plan.n_halo, None)
    odd = lanes() // plan.width % 2 == 1
    for l in range(n):
        for i in range(plan.n_back):
            x = res[l, group(plan.n_outer + 2 * i), :]
            if 2 * i + 1 < plan.n_halo:
                y = res[l, group(plan.n_outer + 2 * i + 1), :]
                x = jnp.where(odd, roll(y, plan.width, 1), x)
            res[l, group(plan.n_outer + i), :] = x
    if b == 0:
        first = plan.n_outer + plan.n_back
        settle(first, plan.n_inner, plan.bins * plan.n_outer, fal, plan.n_speed)
    for k in range(n):
        outs[k][...] = res[me ^ k, pl.ds(0, SUB * plan.back(b)), :]


def deposit_kernel(plan, *refs):
    deposited, (deposit, side, turned) = refs[: plan.bins], refs[plan.bins :]
    n, groups, tiles, width = plan.count, plan.groups, plan.tiles, plan.width
    rows = plan.bins * plan.rows
    for first in range(0, tiles, n):
        held = range(first, min(first + n, tiles))
        for b in range(plan.bins):
            for g in range(groups):
                y = None
                for s, p in enumerate(held):
                    m, v, slot = plan.find(b, p, g)
                    x = roll(deposited[m][group(v), :], (s - slot) * width, 1)
                    y = x if y is None else jnp.where(lanes() < s * width, y, x)
                side[group(b * groups + g), :] = y
        x = side[...].T
        for s, p in enumerate(held):
            turned[pl.ds(p, width, stride=tiles), :rows] = x[s * width : (s + 1) * width]
    lons = tiles * width
    for t in range(-(-lons // LANE)):
        x = turned[pl.ds(LANE * t, LANE), :].T[:rows]
        end = min(LANE * (t + 1), lons)
        for b in range(plan.bins):
            deposit[b, :, LANE * t : end] = x[b * plan.rows : (b + 1) * plan.rows, : end - LANE * t]


def close_kernel(plan, b, ce, cn, ces, cns, far_ces, far_cns, *refs):
    n, groups, tiles = plan.count, plan.groups, plan.tiles
    ins, refs = refs[:n], refs[n:]
    if b:
        shared, refs = refs[:n], refs[n:]
    final = b == plan.bins - 1
    if final:
        before, refs = refs[: b + 1], refs[b + 1 :]
        out, deposit, parts, spread, frame, done, turned, ready, sem = refs
        copies = [
            pltpu.make_async_copy(v, out.at[i], sem.at[tiles + i]) for i, v in enumerate(before[:b])
        ]
        copies.append(pltpu.make_async_copy(before[b], deposit, sem.at[tiles + b]))
        for c in copies:
            c.start()
    else:
        ready, parts, spread, frame, done, turned = refs
    me = lax.axis_index("lev")
    even = lax.axis_index("lat") % 2 == 1
    sub = sublanes()
    own = plan.n_outer + plan.n_back
    for k in range(n):
        if b:
            parts[me ^ k, pl.ds(0, SUB * own), :] = ins[k][...]
            parts[me ^ k, pl.ds(SUB * own, SUB * plan.n_inner), :] = shared[k][
                pl.ds(SUB * own, SUB * plan.n_inner), :
            ]
        else:
            parts[me ^ k] = ins[k][...]
    for p in range(tiles):
        for g in range(groups + 1):
            _, v, slot = plan.find(b, p, g)
            ys = [parts[j, group(v), :] for j in range(n)]
            spread[p, group(g), :] = gather(plan, ys, slot)

    def row_group(g, co, targets):
        q = zonal([spread[p, group(g), :] for p in range(tiles)], co)
        for p in range(tiles):
            for a in targets:
                frame[p, group(a), :] = q[p]

    def core(g):
        co = [[ce[i, p, group(g), :] for i in range(3)] for p in range(tiles + 1)]
        row_group(g, co, (g + 2,))

    loop(groups, core, groups)
    north, south = group(0), group(1)

    def rim(i, p):
        high = jnp.where(even, ces[i, p, north, :], far_ces[i, p, north, :])
        low = jnp.where(even, far_ces[i, p, south, :], ces[i, p, south, :])
        return jnp.where(sub < 4, high, low)

    row_group(groups, [[rim(i, p) for i in range(3)] for p in range(tiles + 1)], (1, groups + 2))
    rows = plan.rows + 2 * SUB

    def body(p):
        low, high = pl.ds(SUB, 2 * SUB), pl.ds(2 * SUB, SUB)
        co = [
            jnp.concatenate(
                [
                    jnp.where(even, far_cns[i, p, low, :], cns[i, p, low, :]),
                    cn[i, p, pl.ds(SUB, plan.rows - SUB), :],
                    jnp.where(even, cns[i, p, high, :], far_cns[i, p, high, :]),
                ],
                0,
            )
            for i in range(3)
        ]
        q, below2, below, beyond = (frame[p, pl.ds(SUB + d, rows), :] for d in (0, -2, -1, 1))
        done[p] = meridional(q, below2, below, beyond, co)[SUB : SUB + plan.rows]

    loop(tiles, body, tiles)
    for p in range(tiles):
        turned[pl.ds(p, LANE, stride=tiles), : plan.rows] = done[p].T
    for t in range(tiles):
        cut = pl.ds(LANE * t, LANE)
        ready[:, cut] = turned[cut, :].T[: plan.rows]
        if final:
            copies.append(pltpu.make_async_copy(ready.at[:, cut], out.at[b, :, cut], sem.at[t]))
            copies[-1].start()
    if final:
        for c in copies:
            c.wait()


def shape(*dims):
    return jax.ShapeDtypeStruct(dims, F32)


def call(kernel, plan, outs, scratch, far_in=False, far_out=False):
    held = pl.BlockSpec(memory_space=pltpu.VMEM)
    far = pl.BlockSpec(memory_space=pltpu.HBM)
    return lambda *args: pl.pallas_call(
        functools.partial(kernel, plan), out_shape=outs, scratch_shapes=scratch,
        in_specs=[far if far_in else held] * len(args),
        out_specs=jax.tree.map(lambda _: far if far_out else held, outs),
        compiler_params=pltpu.CompilerParams(vmem_limit_bytes=VMEM_LIMIT),
    )(*args)


def vmem(*dims):
    return pltpu.VMEM(dims, F32)


def window(tracer, east, north, speed):
    bins, one, rows, lons = tracer.shape
    n, bands = lax.axis_size("lev"), lax.axis_size("lat")
    plan = Plan(bins, rows, lons, n)
    tiles, frame = plan.tiles, rows + 4 * SUB
    tracer, speed = tracer.reshape(bins, rows, lons), speed.reshape(bins, rows, lons)
    east, north = east.reshape(rows, lons), north.reshape(rows, lons)

    assert bins <= 2
    band = shape(tiles, plan.halo_rows, LANE)
    padded = (bins, tiles, rows + 2 * SUB, LANE)
    inputs = [pltpu.with_memory_space_constraint(x, pltpu.HBM) for x in (tracer, east, north, speed)]
    first, second = call(
        rows_kernel, plan, (band, band),
        (
            vmem(2 * plan.halo_rows, lons), vmem(lons, LANE), vmem(bins, 2, SUB, lons),
            pltpu.SemaphoreType.DMA((4 * bins + 4,)),
        ),
        True,
    )(*inputs)
    pairs = [(i, i ^ 1) for i in range(bands) if i ^ 1 < bands]
    first = lax.ppermute(first, "lat", pairs)
    pairs = [(i, ((i + 1) ^ 1) - 1) for i in range(1, bands) if ((i + 1) ^ 1) - 1 < bands]
    second = lax.ppermute(second, "lat", pairs)

    q1, ce, ns, held = call(
        start_kernel, plan,
        (
            shape(*padded), shape(3, tiles + 1, rows, LANE), shape(tiles, rows, LANE),
            shape(bins, rows, lons),
        ),
        (
            vmem(bins * rows, lons), vmem(2 * rows, lons), vmem(2, lons, LANE),
            vmem(tiles, bins * rows, LANE), vmem(tiles, rows, LANE),
            pltpu.SemaphoreType.DMA((bins + 3,)),
        ),
        True,
    )(*inputs)

    def exchanged(parts):
        out = list(parts)
        for k in (*range(2, n), 1):
            out[k] = lax.ppermute(parts[k], "lev", [(i, i ^ k) for i in range(n)])
        return out

    zs, q4, cn = call(
        inner_kernel, plan,
        (shape(HSUB - 1, *padded), shape(bins, tiles, rows, LANE), shape(3, tiles, rows, LANE)),
        (vmem(*padded),),
    )(q1, ce, ns)

    early = SUB * (plan.n_speed + plan.n_inner)
    part = shape(early, LANE)
    speeds = exchanged(
        call(
            speed_kernel, plan, (part,) * n,
            (
                vmem(lons, LANE), vmem(tiles, bins * rows, LANE),
                vmem(n, early, LANE),
            ),
        )(held.reshape(bins * rows, lons), q4),
    )

    rim = (
        shape(3, tiles + 1, 2 * SUB, LANE), shape(3, tiles, 4 * SUB, LANE),
        shape(bins, tiles, SUB, LANE),
    )
    side = vmem(bins, tiles, 6 * SUB, LANE)
    near, ces, cns, fhs = call(
        near_kernel, plan, (shape(bins, tiles, 3 * SUB, LANE),) + rim, (side, side)
    )(second, q1, zs, ce, ns)

    part = shape(SUB * (plan.n_outer + plan.n_halo), LANE)
    every = vmem(n, SUB * (plan.n_outer + plan.n_halo), LANE)
    side = vmem(1, tiles, 6 * SUB, LANE)
    fields, shared = [], ()
    for b in range(bins):
        made = call(
            lambda plan, *refs, b=b: far_kernel(plan, b, *refs), plan,
            (part,) * n + (() if b else (rim[2], rim[0], rim[1])),
            (side, side, vmem(1, tiles, 3 * SUB, LANE), every),
        )(first, q1, zs, q4, ce, ns, near, fhs, *shared)
        shared = shared or tuple(made[n:])
        fields.append(exchanged(made[:n]))
    _, far_ces, far_cns = shared
    deposited, settled = [], []
    for b in range(bins):
        total, *parts = call(
            lambda plan, *refs, b=b: settle_kernel(plan, b, *refs), plan,
            (shape(SUB * plan.back(b), LANE),) * (n + 1),
            (
                every, vmem(n, early, LANE),
                vmem(n, SUB * (plan.n_outer + plan.n_halo + plan.n_inner), LANE),
            ),
        )(*fields[b], *speeds)
        deposited.append(total)
        settled.append(exchanged(parts))
    local = tiles * plan.width
    deposit = call(
        deposit_kernel, plan, shape(bins, rows, local),
        (vmem(bins * rows, LANE), vmem(-(-local // LANE) * LANE, LANE)),
    )(*deposited)

    done = []
    for b in range(bins):
        final = b == bins - 1
        scratch = (
            vmem(n, SUB * plan.back(0), LANE), vmem(tiles, rows + SUB, LANE), vmem(tiles, frame, LANE),
            vmem(tiles, rows, LANE), vmem(lons, LANE),
        )
        if final:
            outs = shape(bins, rows, lons), shape(bins, rows, local)
            scratch += vmem(rows, lons), pltpu.SemaphoreType.DMA((tiles + bins,))
        done.append(
            call(
                lambda plan, *refs, b=b: close_kernel(plan, b, *refs), plan,
                outs if final else shape(rows, lons), scratch, False, final,
            )(
                ce, cn, ces, cns, far_ces, far_cns, *settled[b], *(settled[0] if b else ()),
                *((*done, deposit) if final else ()),
            )
        )
    out, deposit = done[-1]
    return out.reshape(bins, one, rows, lons), deposit


def solution(mesh):
    in_specs = (
        P(None, "lev", "lat", None),
        P("lev", "lat", None),
        P("lev", "lat", None),
        P(None, "lev", "lat", None),
    )
    out_specs = (P(None, "lev", "lat", None), P(None, "lat", "lev"))
    return jax.shard_map(window, mesh=mesh, in_specs=in_specs, out_specs=out_specs, check_vma=False)
```
